32 devices in a mesh: macro: 8 (over y, x, core), rve: 4 (over z).
Axes of the slice: x: 2, y: 2, z: 4, core: 2. Of those that a mesh axis runs over, the one named last changes fastest.
Arguments:
- deform: float32 [9, 512], P(None, 'macro'), may hold values from -6 to 6
- plastic: int32 [512], P('macro'), may hold values 0 or 1
- route: int32 [512], P('macro'), may hold values from 0 to 7, as said below
- stiff: float32 [8, 1536], P('macro', 'rve'), may hold values from 0.1 to 2
- cubic: float32 [8, 1536], P('macro', 'rve'), may hold values from 0.5 to 5
- coupling: float32 [8, 24, 2, 64, 64], P('macro', 'rve'), may hold values from -0.75 to 0.75
- conn: int32 [8, 24, 2], P('macro', 'rve'), may hold values from 0 to 5
- iface: float32 [8, 256, 64], P('macro', 'rve'), may hold values from -0.75 to 0.75
- load_map: float32 [8, 9, 1536], P('macro', None, 'rve'), may hold values from -2 to 2
- average_map: float32 [8, 9, 1536], P('macro', None, 'rve'), may hold values from -0.15625 to 0.15625
Outputs:
- stress: float32 [9, 512], P(None, 'macro')
- micro_field: float32 [8, 1536, 128], P('macro', 'rve')
The draws below stay inside these ranges and needn't reach their ends.
Inputs may be any that keep to these rules, and one draw needn't show every extreme that they name: `route`: among the points of one macro section no group is named more than 16 times, and one group is named exactly 16 times by every section. `conn`: an index among the 6 blocks held with the same block row on one device.
All inputs are finite; a program needn't handle non-finite values. No bound on the sum of `plastic` on one device may be relied on, other than what follows from the above.
Results may differ from the reference program's by a relative error of at most 0.0003.
Values sent between devices are 32-bit elements; how exact they have to be, the bound alone decides.
A program may use at most 64 MiB of HBM per device.

```python
import math
import jax
import jax.numpy as jnp
from jax import lax

POINTS_SEC = 64
BLOCKS_DEV = 6
BLOCK = 64
SLOTS = 2
ITERS = 2
NEWTON = 2
GROUPS = 8
CAPACITY = 16
GROUP_SLOTS = 128
POINTS = 512
DOFS_DEV = 384
RVE_BLOCKS = 24
RVE_DOFS = 1536
N_RVE = 4


def draw_route(key, part):
    chosen = jax.random.randint(jax.random.fold_in(key, 1), (), 0, GROUPS).astype(jnp.int32)
    others = jnp.arange((GROUPS - 1) * CAPACITY, dtype=jnp.int32) // CAPACITY
    others = others + (others >= chosen).astype(jnp.int32)

    def one_section(section):
        section_key = jax.random.fold_in(jax.random.fold_in(key, 2), section)
        shuffled = jax.random.permutation(jax.random.fold_in(section_key, 1), others)
        section_rows = jnp.concatenate([jnp.zeros((CAPACITY,), jnp.int32) + chosen, shuffled[:POINTS_SEC - CAPACITY]])
        return jax.random.permutation(jax.random.fold_in(section_key, 2), section_rows)
    return jax.vmap(one_section)(jnp.arange(GROUPS, dtype=jnp.int32)).reshape(POINTS_SEC * GROUPS)


def set_ends(drawn, stream_key, smallest, top_value):
    dims = drawn.shape
    place = [jax.random.randint(jax.random.fold_in(stream_key, axis), (), 0, dims[axis]) for axis in range(len(dims))]
    drawn = drawn.at[tuple(place)].set(smallest)
    longest = dims.index(max(dims))
    place[longest] = (place[longest] + 1) % dims[longest]
    return drawn.at[tuple(place)].set(top_value)


def shard_levels(stream_key, dims, cuts, least, high):
    level, own = 1.0, jax.random.fold_in(stream_key, 6)
    for dim, parts in cuts:
        draws = jnp.exp(jax.random.uniform(jax.random.fold_in(own, dim), (parts,), jnp.float32, least / len(cuts), high / len(cuts)))
        level = level * jnp.repeat(draws, dims[dim] // parts).reshape([-1 if axis == dim else 1 for axis in range(len(dims))])
    return level


def noise(rng, shape, scale, reach, pieces=(), kind=jnp.bfloat16):
    values = jax.random.normal(rng, shape, jnp.float32) * scale
    if len(pieces) > 0:
        values = shard_levels(rng, shape, pieces, -0.22, 0.18) * values
    return jnp.clip(values, min=-reach, max=reach).astype(kind)


def setup_inputs(seed: int = 0) -> dict:
    key_of = jax.random.split(jax.random.key(seed), 11)
    return {
        "deform": noise(key_of[0], (9, POINTS), 1.0, 6.0, ((1, 8),), jnp.float32),
        "plastic": set_ends((jax.random.randint(key_of[1], (POINTS,), 0, 2) < 1).astype(jnp.int32), jax.random.fold_in(key_of[1], 1), 0, 1),
        "route": draw_route(jax.random.fold_in(key_of[10], 71), 0),
        "stiff": jnp.clip(jnp.exp(math.log(2.0) - 2.9957323 * jax.random.uniform(key_of[3], (GROUPS, RVE_DOFS), jnp.float32) ** shard_levels(key_of[3], (GROUPS, RVE_DOFS), ((0, 8), (1, 4)), -0.2, 0.2)), 0.1, 2.0),
        "cubic": jnp.clip(jnp.exp(math.log(5.0) - 2.3025851 * jax.random.uniform(key_of[4], (GROUPS, RVE_DOFS), jnp.float32) ** shard_levels(key_of[4], (GROUPS, RVE_DOFS), ((0, 8), (1, 4)), -0.2, 0.2)), 0.5, 5.0),
        "coupling": noise(key_of[5], (GROUPS, RVE_BLOCKS, SLOTS, BLOCK, BLOCK), BLOCK ** -0.5, 0.75, ((0, 8), (1, 4)), jnp.float32),
        "conn": set_ends(jax.random.randint(key_of[6], (GROUPS, RVE_BLOCKS, SLOTS), 0, BLOCKS_DEV), jax.random.fold_in(key_of[6], 1), 0, BLOCKS_DEV - 1).astype(jnp.int32),
        "iface": noise(key_of[7], (GROUPS, N_RVE * BLOCK, BLOCK), BLOCK ** -0.5, 0.75, ((0, 8), (1, 4)), jnp.float32),
        "load_map": noise(key_of[8], (GROUPS, 9, RVE_DOFS), 9 ** -0.5, 2.0, ((0, 8), (2, 4)), jnp.float32),
        "average_map": noise(key_of[9], (GROUPS, 9, RVE_DOFS), RVE_DOFS ** -0.5, 0.15625, ((0, 8), (2, 4)), jnp.float32),
    }


HIGHEST_PREC = lax.Precision.HIGHEST
EPSILON = 1e-6


def slot_index(route_rows, capacity):
    point_count = route_rows.shape[0]
    position = jnp.arange(point_count, dtype=jnp.int32)
    same_group = route_rows[:, None] == route_rows[None, :]
    before = position[None, :] < position[:, None]
    rank_in = jnp.sum(jnp.where(jnp.logical_and(same_group, before), 1, 0).astype(jnp.int32), axis=1)
    return route_rows * capacity + rank_in


def local_matrix(coupling, conn, stiff):
    blocks, slot_count, block_size, _ = coupling.shape
    spring = jnp.einsum("bsxk,bsyk->bsxy", coupling, coupling, precision=HIGHEST_PREC)
    block_ids = jnp.arange(blocks, dtype=jnp.int32)
    own_mark = (block_ids[None, None, :] == block_ids[:, None, None]).astype(jnp.float32)
    far_mark = jnp.logical_and(block_ids[None, None, :] == conn[:, :, None], conn[:, :, None] != block_ids[:, None, None]).astype(jnp.float32)
    weight = own_mark - far_mark
    pair_mark = jnp.einsum("bsk,bsl->bskl", weight, weight, precision=HIGHEST_PREC)
    assembled = jnp.einsum("bskl,bsxy->kxly", pair_mark, spring, precision=HIGHEST_PREC)
    assembled = assembled.reshape(blocks * block_size, blocks * block_size)
    return assembled + jnp.diag(stiff)


def solve_group(items):
    strain, flag_row, stiff, cubic, coupling, conn, iface, load_map, average_map = items
    part_count = N_RVE
    local_parts = jax.vmap(local_matrix)(coupling.reshape(part_count, BLOCKS_DEV, SLOTS, BLOCK, BLOCK), conn.reshape(part_count, BLOCKS_DEV, SLOTS), stiff.reshape(part_count, DOFS_DEV))
    edge_blocks = iface.reshape(part_count, BLOCK, BLOCK)
    springs = jnp.einsum("qxk,qyk->qxy", edge_blocks, edge_blocks, precision=HIGHEST_PREC)
    next_springs = jnp.roll(springs, -1, axis=0)
    load_cols = jnp.einsum("ci,cp->ip", load_map, strain, precision=HIGHEST_PREC).reshape(part_count, DOFS_DEV, GROUP_SLOTS)
    hard = flag_row[None, None, :] * cubic.reshape(part_count, DOFS_DEV, 1)

    def operate(field):
        product = jnp.einsum("qij,qjp->qip", local_parts, field, precision=HIGHEST_PREC)
        first_rows = field[:, :BLOCK]
        last_rows = field[:, -BLOCK:]
        prev_last = jnp.roll(last_rows, 1, axis=0)
        next_first = jnp.roll(first_rows, -1, axis=0)
        top_flux = jnp.einsum("qij,qjp->qip", springs, first_rows - prev_last, precision=HIGHEST_PREC)
        bottom = jnp.einsum("qij,qjp->qip", next_springs, last_rows - next_first, precision=HIGHEST_PREC)
        product = product.at[:, :BLOCK].add(top_flux)
        product = product.at[:, -BLOCK:].add(bottom)
        return product

    def col_sum(values):
        return jnp.sum(values, axis=(0, 1))

    solution = jnp.zeros_like(load_cols)
    for newton_step in range(NEWTON):
        tangent_add = 3.0 * hard * solution * solution
        right_side = load_cols - operate(solution) - hard * (solution * solution * solution)

        def sweep(turn_index, carried):
            iterate, residue, direct, norm_now = carried
            product = operate(direct) + tangent_add * direct
            step_len = norm_now / (col_sum(direct * product) + EPSILON)
            iterate = iterate + step_len * direct
            residue = residue - step_len * product
            norm_next = col_sum(residue * residue)
            direct = residue + (norm_next / (norm_now + EPSILON)) * direct
            return iterate, residue, direct, norm_next

        start = (jnp.zeros_like(right_side), right_side, right_side, col_sum(right_side * right_side))
        iterate, residue, direct, norm_now = lax.fori_loop(0, ITERS, sweep, start)
        solution = solution + iterate
    field_flat = solution.reshape(RVE_DOFS, GROUP_SLOTS)
    group_stress = jnp.einsum("ci,ip->cp", average_map, field_flat, precision=HIGHEST_PREC)
    return group_stress, field_flat


def partial_slot(route_rows):
    return slot_index(route_rows, CAPACITY)


def reference(deform, plastic, route, stiff, cubic, coupling, conn, iface, load_map, average_map):
    sections = GROUPS
    route_sec = route.reshape(sections, POINTS_SEC)
    slot_ids = jax.vmap(partial_slot)(route_sec)
    places = jnp.arange(GROUPS * CAPACITY, dtype=jnp.int32)
    select = (slot_ids[:, :, None] == places[None, None, :]).astype(jnp.float32)
    deform_sec = deform.reshape(9, sections, POINTS_SEC)
    sent = jnp.einsum("cmi,mis->cms", deform_sec, select, precision=HIGHEST_PREC).reshape(9, sections, GROUPS, CAPACITY)
    received = jnp.transpose(sent, (2, 0, 1, 3)).reshape(GROUPS, 9, GROUP_SLOTS)
    flag_sec = plastic.reshape(sections, POINTS_SEC).astype(jnp.float32)
    flag_sent = jnp.einsum("mi,mis->ms", flag_sec, select, precision=HIGHEST_PREC).reshape(sections, GROUPS, CAPACITY)
    received_flag = jnp.transpose(flag_sent, (1, 0, 2)).reshape(GROUPS, GROUP_SLOTS)
    group_stress, micro_field = lax.map(solve_group, (received, received_flag, stiff, cubic, coupling, conn, iface, load_map, average_map))
    stress_cols = jnp.transpose(group_stress, (1, 0, 2)).reshape(9, GROUPS, sections, CAPACITY)
    stress_sec = jnp.transpose(stress_cols, (0, 2, 1, 3)).reshape(9, sections, GROUPS * CAPACITY)
    stress = jnp.einsum("cms,mis->cmi", stress_sec, select, precision=HIGHEST_PREC).reshape(9, POINTS)
    return stress, micro_field
```

```python
import functools

import jax
import jax.numpy as jnp
from jax import lax
from jax.experimental import pallas as pl
from jax.experimental.pallas import tpu as pltpu
from jax.sharding import PartitionSpec as P

EPSILON = 1e-06
MESH = pl.DeviceIdType.MESH
HIGHEST = lax.Precision.HIGHEST
F32 = jnp.float32
BF16 = jnp.bfloat16
LANES = 128
NT = (((1,), (1,)), ((), ()))


def split(values):
    high = values.astype(BF16)
    return high, (values - high.astype(F32)).astype(BF16)


def dot(left, right):
    return jnp.dot(left, right, preferred_element_type=F32)


def dot_nt(left, right, precision=None):
    return lax.dot_general(left, right, NT, precision=precision, preferred_element_type=F32)


def apply_split(high, low, values):
    value_high, value_low = split(values)
    width = values.shape[1]
    wide = dot(high, jnp.concatenate([value_high, value_low], axis=1))
    return wide[:, :width] + wide[:, width:] + dot(low, value_high)


def apply_rows(values, high, low):
    value_high, value_low = split(values)
    rows = values.shape[0]
    tall = dot(jnp.concatenate([value_high, value_low], axis=0), high)
    return tall[:rows] + tall[rows:] + dot(value_high, low)


def square_nt(values):
    high, low = split(values)
    return dot_nt(high, high) + (dot_nt(high, low) + dot_nt(low, high))


def iota(shape, dim):
    return lax.broadcasted_iota(jnp.int32, shape, dim)


def pad_rows(values, rows):
    missing = rows - values.shape[0]
    if missing == 0:
        return values
    return jnp.concatenate([values, jnp.zeros((missing, values.shape[1]), values.dtype)], axis=0)


def col_sum(values):
    return jnp.sum(values, axis=0, keepdims=True)


def kernel(
    groups, parts, capacity,
    deform_hbm, plastic_hbm, route_hbm, stiff_hbm, cubic_hbm, coupling_hbm, conn_ref,
    iface_hbm, load_hbm, average_hbm,
    stress_ref, field_ref,
    deform_ref, plastic_ref, route_ref, stiff_ref, cubic_ref, coupling_ref,
    iface_ref, load_ref, average_ref,
    whole, stiff_high, stiff_low,
    out_points, in_points, edge_out, edge_in,
    halo_out, halo_in, gram_buf, first_buf, mean_buf, second_buf, out_rows, in_rows, field_buf,
    input_sem, output_sem,
    point_send, point_recv, edge_send, edge_recv, halo_send, halo_recv,
    gram_send, gram_recv, first_send, first_recv, mean_send, mean_recv, second_send, second_recv, row_send, row_recv,
):
    group = lax.axis_index("macro")
    part = lax.axis_index("rve")
    blocks, slots, block = coupling_ref.shape[1], coupling_ref.shape[2], coupling_ref.shape[3]
    dofs = blocks * block
    comps, points = deform_ref.shape
    padded = out_points.shape[1]
    columns = groups * capacity
    places = groups * padded

    barrier = pltpu.get_barrier_semaphore()
    for step in range(1, parts):
        pl.semaphore_signal(
            barrier, inc=1, device_id={"rve": lax.rem(part + step, parts)}, device_id_type=MESH
        )
    for step in range(1, groups):
        pl.semaphore_signal(
            barrier, inc=1, device_id={"macro": lax.rem(group + step, groups)}, device_id_type=MESH
        )

    loads = []
    for source, target in (
        (coupling_hbm, coupling_ref), (iface_hbm, iface_ref), (load_hbm, load_ref),
        (cubic_hbm, cubic_ref), (stiff_hbm, stiff_ref), (deform_hbm, deform_ref),
        (plastic_hbm, plastic_ref), (route_hbm, route_ref), (average_hbm, average_ref),
    ):
        loads.append(pltpu.make_async_copy(source, target, input_sem.at[len(loads)]))
        loads[-1].start()
    coupling_load, iface_load = loads[:2]
    early_loads, late_loads = loads[2:5], loads[5:]

    def exchange(source, target, send, recv):
        copies = []
        for step in range(1, groups):
            peer = lax.rem(group + step, groups)
            copies.append(pltpu.make_async_remote_copy(
                src_ref=source.at[peer], dst_ref=target.at[group],
                send_sem=send.at[step - 1], recv_sem=recv.at[step - 1],
                device_id={"macro": peer}, device_id_type=MESH,
            ))
            copies[-1].start()
        return copies

    def share(buffer, send, recv):
        copies = []
        for step in range(1, parts):
            copies.append(pltpu.make_async_remote_copy(
                src_ref=buffer.at[part], dst_ref=buffer.at[part],
                send_sem=send.at[step - 1], recv_sem=recv.at[step - 1],
                device_id={"rve": lax.rem(part + step, parts)}, device_id_type=MESH,
            ))
            copies[-1].start()
        return copies

    after, behind = lax.rem(part + 1, parts), lax.rem(part + parts - 1, parts)

    def to_neighbours(first, last, target, send, recv):
        copies = []
        for place, (source, peer) in enumerate(((last, after), (first, behind))):
            copies.append(pltpu.make_async_remote_copy(
                src_ref=source, dst_ref=target.at[place],
                send_sem=send.at[place], recv_sem=recv.at[place],
                device_id={"rve": peer}, device_id_type=MESH,
            ))
            copies[-1].start()
        return copies

    def arrive(copies):
        for copy in copies:
            copy.wait_recv()

    def gathered(buffer):
        total = buffer[0]
        for other in range(1, parts):
            total = total + buffer[other]
        return total

    coupling_load.wait()
    lane = iota((block, LANES), 1) < block
    doubled = []
    for row in range(blocks):
        square = square_nt(coupling_ref[0, row].reshape(slots * block, block))
        doubled.append([])
        for slot in range(slots):
            spring = square[slot * block:(slot + 1) * block, slot * block:(slot + 1) * block]
            doubled[row].append(jnp.concatenate([spring, spring], axis=1))

    def mark(row, slot, far):
        if row == far:
            return jnp.float32(0.0)
        return jnp.where(conn_ref[0, slot, row] == far, 1.0, 0.0).astype(F32)

    for row in range(blocks):
        own = doubled[row][0]
        for slot in range(1, slots):
            own = own + doubled[row][slot]
        for other in range(blocks):
            if other != row:
                for slot in range(slots):
                    own = own + doubled[other][slot] * mark(other, slot, row)
        for pair in range(blocks // 2):
            left, right = 2 * pair, 2 * pair + 1
            value = jnp.zeros((block, LANES), F32)
            for slot in range(slots):
                value = value - doubled[row][slot] * jnp.where(
                    lane, mark(row, slot, left), mark(row, slot, right)
                )
                value = value - jnp.where(
                    lane, doubled[left][slot] * mark(left, slot, row),
                    doubled[right][slot] * mark(right, slot, row),
                )
            if row == left:
                value = value + jnp.where(lane, own, 0.0)
            if row == right:
                value = value + jnp.where(lane, 0.0, own)
            whole[row * block:(row + 1) * block, pair * LANES:(pair + 1) * LANES] = value

    iface_load.wait()
    for copy in early_loads:
        copy.wait()
    own_edge = iface_ref[0]
    own_spring = square_nt(own_edge)
    own_high, own_low = split(own_spring)
    diagonal = iota((dofs, dofs), 0) == iota((dofs, dofs), 1)
    stiffness = whole[...] + jnp.where(diagonal, stiff_ref[...], 0.0)
    high, low = split(stiffness)
    stiff_high[...] = high
    stiff_low[...] = low
    high, low = split(stiffness[:block, :block] + own_spring)
    stiff_high[:block, :block] = high
    stiff_low[:block, :block] = low

    maps = pad_rows(load_ref[:, 0, :], 16)
    cubic = pad_rows(cubic_ref[...], 16)

    def ends(values):
        return jnp.concatenate([values[:, :block], values[:, dofs - block:]], axis=1)

    image_map = apply_rows(maps, stiff_high[...], stiff_low[...])
    packed_rows = edge_out.shape[0] - block // 2
    edge_out[:packed_rows, :] = pad_rows(
        ends(jnp.concatenate([maps[:comps], image_map[:comps], cubic[:1]], axis=0)), packed_rows
    )
    edge_out[packed_rows:, :] = jnp.concatenate([own_edge[:block // 2], own_edge[block // 2:]], axis=1)

    pl.semaphore_wait(barrier, groups + parts - 2)

    sends = []
    edge_copies = to_neighbours(edge_out, edge_out, edge_in, edge_send, edge_recv)

    for copy in late_loads:
        copy.wait()
    route = route_ref[...]
    hot = (iota((groups, points), 0) == route).astype(F32)
    before = (iota((points, points), 0) < iota((points, points), 1)).astype(BF16)
    rank = col_sum(hot * dot(hot.astype(BF16), before))
    slot_of = (route * padded).astype(F32) + rank
    select = (iota((places, points), 0).astype(F32) == slot_of).astype(F32)
    sent = pad_rows(
        jnp.concatenate([deform_ref[...], plastic_ref[...].astype(F32)], axis=0), LANES
    )
    outgoing = dot_nt(select, sent, HIGHEST)
    out_points[...] = outgoing.reshape(groups, padded, LANES)
    point_copies = exchange(out_points, in_points, point_send, point_recv)
    sends += point_copies + edge_copies
    in_points[group] = out_points[group]
    average_high, average_low = split(pad_rows(average_ref[:, 0, :], 16))

    arrive(edge_copies)
    packed = edge_in[1, packed_rows:, :]
    next_spring = square_nt(jnp.concatenate([packed[:, :block], packed[:, block:]], axis=0))
    next_high, next_low = split(next_spring)
    high, low = split(stiffness[dofs - block:, dofs - block:] + next_spring)
    stiff_high[dofs - block:, dofs - block:] = high
    stiff_low[dofs - block:, dofs - block:] = low

    def own_rows(values):
        return apply_rows(values, own_high, own_low)

    def next_rows(values):
        return apply_rows(values, next_high, next_low)

    def unpack(values):
        return jnp.concatenate([
            pad_rows(values[:comps], 16), pad_rows(values[comps:2 * comps], 16),
            pad_rows(values[2 * comps:2 * comps + 1], 16),
        ], axis=0)

    prev_edge, next_edge = unpack(edge_in[0, :packed_rows]), unpack(edge_in[1, :packed_rows])
    prev_map, next_map = prev_edge[0:16, block:], next_edge[0:16, :block]
    first_map, last_map = maps[:, :block], maps[:, dofs - block:]
    through_own = own_rows(jnp.concatenate([prev_map, first_map], axis=0))
    through_next = next_rows(jnp.concatenate([next_map, last_map], axis=0))
    prev_image = prev_edge[16:32, block:] + through_own[:16] - through_own[16:]
    next_image = next_edge[16:32, :block] - through_next[16:]
    image_map = jnp.concatenate([
        image_map[:, :block] - through_own[:16],
        image_map[:, block:dofs - block],
        image_map[:, dofs - block:] + through_next[16:] - through_next[:16],
    ], axis=1)
    second_map = apply_rows(image_map, stiff_high[...], stiff_low[...])
    second_map = jnp.concatenate([
        second_map[:, :block] - own_rows(prev_image),
        second_map[:, block:dofs - block],
        second_map[:, dofs - block:] - next_rows(next_image),
    ], axis=1)
    basis = jnp.concatenate([maps, image_map, second_map, cubic], axis=0)
    products = dot_nt(basis[0:32], basis[0:48], HIGHEST)
    gram_buf[part, 0:16] = jnp.concatenate(
        [products[0:16, 0:32], products[16:32, 16:48], jnp.zeros((16, LANES - 64), F32)], axis=1
    )
    gram_buf[part, 16:32] = ends(second_map)
    gram_copies = share(gram_buf, gram_send, gram_recv)
    sends += gram_copies

    basis_cols = jnp.transpose(basis)
    arrive(point_copies)

    def compact(rows):
        rows = rows.reshape(places, LANES)
        if padded == capacity:
            return rows
        row, col = iota((columns, places), 0), iota((columns, places), 1)
        take = (col == (row // capacity) * padded + row % capacity).astype(F32)
        return jnp.dot(take, rows, precision=HIGHEST, preferred_element_type=F32)

    received = jnp.transpose(compact(in_points[...]))[:16]
    flag = received[comps:comps + 1]
    strain = jnp.where(iota((16, columns), 0) < comps, received, 0.0)
    hard = basis_cols[:, 48:49] * flag

    arrive(gram_copies)
    ghost_basis = jnp.concatenate([
        jnp.concatenate([prev_map, next_map], axis=1),
        jnp.concatenate([prev_image, next_image], axis=1),
        jnp.concatenate(
            [gram_buf[behind, 16:32][:, block:], gram_buf[after, 16:32][:, :block]], axis=1
        ),
        jnp.concatenate([prev_edge[32:48, block:], next_edge[32:48, :block]], axis=1),
    ], axis=0)
    ghost_cols = jnp.transpose(ghost_basis)
    ghost_hard = ghost_cols[:, 48:49] * flag
    gram = gathered(gram_buf)
    forms = jnp.concatenate(
        [gram[0:16, 0:16], gram[0:16, 16:32], gram[0:16, 32:48], gram[0:16, 48:64]], axis=0
    )
    forms = jnp.dot(forms, strain, precision=HIGHEST, preferred_element_type=F32)
    norm = col_sum(forms[0:16] * strain)
    curve = col_sum(forms[16:32] * strain)
    third = col_sum(forms[32:48] * strain)
    fourth = col_sum(forms[48:64] * strain)

    def second_step(norm, curve, left_norm, left_curve, cross):
        ratio = left_norm / (norm + EPSILON)
        next_curve = left_curve + ratio * (2.0 * cross + ratio * curve)
        next_curve = jnp.maximum(next_curve, 0.09 * left_norm)
        next_len = left_norm / (next_curve + EPSILON)
        return next_len, next_len * ratio

    step_len = norm / (curve + EPSILON)
    left_norm = jnp.maximum(norm - step_len * (2.0 * curve - step_len * third), 0.0)
    left_curve = curve - step_len * (2.0 * third - step_len * fourth)
    cross = curve - step_len * third
    next_len, carried = second_step(norm, curve, left_norm, left_curve, cross)
    along = step_len + carried + next_len
    across = next_len * step_len
    zero = jnp.zeros_like(strain)
    weights = jnp.concatenate([
        jnp.concatenate([along * strain, -across * strain, zero], axis=0),
        jnp.concatenate([strain, -along * strain, across * strain], axis=0),
    ], axis=1)
    both = jnp.dot(
        jnp.concatenate([basis_cols[:, :48], ghost_cols[:, :48]], axis=0), weights,
        precision=HIGHEST, preferred_element_type=F32,
    )
    solved = both[:dofs, :columns]
    hard_square = hard * solved * solved
    tangent = 3.0 * hard_square
    residue = both[:dofs, columns:] - hard_square * solved
    ghost_solved = both[dofs:, :columns]
    ghost = both[dofs:, columns:] - ghost_hard * ghost_solved * ghost_solved * ghost_solved

    def coupled(product, ghost):
        top = product[:block] - apply_split(own_high, own_low, ghost[:block])
        bottom = product[dofs - block:] - apply_split(next_high, next_low, ghost[block:])
        return jnp.concatenate([top, product[block:dofs - block], bottom], axis=0)

    def averaged(values):
        return apply_split(average_high, average_low, values)[:comps]

    image = coupled(apply_split(stiff_high[...], stiff_low[...], residue), ghost)
    image = image + tangent * residue
    first_buf[part] = pad_rows(jnp.concatenate([
        col_sum(residue * residue), col_sum(residue * image),
    ], axis=0), first_buf.shape[1])
    first_copies = share(first_buf, first_send, first_recv)
    halo_out[0] = image[:block]
    halo_out[1] = image[dofs - block:]
    halo_copies = to_neighbours(
        halo_out.at[0], halo_out.at[1], halo_in, halo_send, halo_recv
    )
    second = apply_split(stiff_high[...], stiff_low[...], image)
    mean_buf[part] = pad_rows(jnp.concatenate(
        [averaged(solved), averaged(residue), averaged(image)], axis=0
    ), mean_buf.shape[1])
    mean_copies = share(mean_buf, mean_send, mean_recv)
    sends += halo_copies + first_copies + mean_copies
    arrive(first_copies)
    sums = gathered(first_buf)
    norm, curve = sums[0:1], sums[1:2]
    step_len = norm / (curve + EPSILON)
    left = residue - step_len * image
    arrive(halo_copies)
    second = coupled(second, halo_in[...].reshape(2 * block, columns)) + tangent * image
    left_image = image - step_len * second
    second_buf[part] = pad_rows(jnp.concatenate(
        [col_sum(left * left), col_sum(left * left_image), col_sum(left * image)], axis=0
    ), 8)
    second_copies = share(second_buf, second_send, second_recv)
    sends += second_copies
    arrive(mean_copies)
    means = gathered(mean_buf)
    arrive(second_copies)
    last = gathered(second_buf)
    next_len, carried = second_step(norm, curve, last[0:1], last[1:2], last[2:3])
    along = step_len + carried
    total = (
        means[:comps] + along * means[comps:2 * comps]
        + next_len * (means[comps:2 * comps] - step_len * means[2 * comps:3 * comps])
    )

    rows = jnp.transpose(pad_rows(total, LANES))
    if padded != capacity:
        row, col = iota((places, columns), 0), iota((places, columns), 1)
        spread = jnp.logical_and(
            col == (row // padded) * capacity + row % padded, row % padded < capacity
        ).astype(F32)
        rows = jnp.dot(spread, rows, precision=HIGHEST, preferred_element_type=F32)
    out_rows[...] = rows.reshape(groups, padded, LANES)
    row_copies = exchange(out_rows, in_rows, row_send, row_recv)
    sends += row_copies
    in_rows[group] = out_rows[group]
    field_buf[0] = solved + along * residue + next_len * left
    field_ref[...] = field_buf[...]
    arrive(row_copies)
    back = jnp.transpose(in_rows[...].reshape(places, LANES))[:16]
    picked = jnp.dot(back, select, precision=HIGHEST, preferred_element_type=F32)
    stress_ref[...] = picked[:comps]
    for copy in sends:
        copy.wait_send()


def solution(mesh):
    groups, parts = mesh.shape["macro"], mesh.shape["rve"]

    def shards(deform, plastic, route, stiff, cubic, coupling, conn, iface, load_map, average_map):
        comps, points = deform.shape
        blocks, block = coupling.shape[1], coupling.shape[3]
        dofs = blocks * block
        capacity = 2 * points // groups
        columns = groups * capacity
        padded = -(-capacity // 8) * 8
        edge_rows = -(-(2 * comps + 1) // 8) * 8
        vmem = pl.BlockSpec(memory_space=pltpu.VMEM)
        hbm = pl.BlockSpec(memory_space=pltpu.HBM)
        dma = pltpu.SemaphoreType.DMA
        return pl.pallas_call(
            functools.partial(kernel, groups, parts, capacity),
            out_shape=(
                pltpu.VMEM((comps, points), F32),
                pltpu.VMEM((1, dofs, columns), F32),
            ),
            in_specs=[hbm] * 6 + [pl.BlockSpec(memory_space=pltpu.SMEM)] + [hbm] * 3,
            out_specs=(vmem, vmem),
            scratch_shapes=[
                pltpu.VMEM(deform.shape, F32),
                pltpu.VMEM((1, points), jnp.int32),
                pltpu.VMEM((1, points), jnp.int32),
                pltpu.VMEM((1, dofs), F32),
                pltpu.VMEM((1, dofs), F32),
                pltpu.VMEM(coupling.shape, F32),
                pltpu.VMEM(iface.shape, F32),
                pltpu.VMEM((comps, 1, dofs), F32),
                pltpu.VMEM((comps, 1, dofs), F32),
                pltpu.VMEM((dofs, dofs), F32),
                pltpu.VMEM((dofs, dofs), BF16),
                pltpu.VMEM((dofs, dofs), BF16),
                pltpu.VMEM((groups, padded, LANES), F32),
                pltpu.VMEM((groups, padded, LANES), F32),
                pltpu.VMEM((edge_rows + block // 2, LANES), F32),
                pltpu.VMEM((2, edge_rows + block // 2, LANES), F32),
                pltpu.VMEM((2, block, columns), F32),
                pltpu.VMEM((2, block, columns), F32),
                pltpu.VMEM((parts, 32, LANES), F32),
                pltpu.VMEM((parts, 8, columns), F32),
                pltpu.VMEM((parts, 32, columns), F32),
                pltpu.VMEM((parts, 8, columns), F32),
                pltpu.VMEM((groups, padded, LANES), F32),
                pltpu.VMEM((groups, padded, LANES), F32),
                pltpu.VMEM((1, dofs, columns), F32),
                dma((9,)), dma,
                dma((groups - 1,)), dma((groups - 1,)),
                dma((2,)), dma((2,)),
                dma((2,)), dma((2,)),
                dma((parts - 1,)), dma((parts - 1,)),
                dma((parts - 1,)), dma((parts - 1,)),
                dma((parts - 1,)), dma((parts - 1,)),
                dma((parts - 1,)), dma((parts - 1,)),
                dma((groups - 1,)), dma((groups - 1,)),
            ],
            compiler_params=pltpu.CompilerParams(
                collective_id=0, has_side_effects=True, vmem_limit_bytes=60 * 1024 * 1024
            ),
        )(
            deform, plastic[None], route[None], stiff, cubic, coupling,
            jnp.transpose(conn, (0, 2, 1)), iface,
            jnp.transpose(load_map, (1, 0, 2)), jnp.transpose(average_map, (1, 0, 2)),
        )

    return jax.shard_map(
        shards,
        mesh=mesh,
        in_specs=(
            P(None, "macro"),
            P("macro"),
            P("macro"),
            P("macro", "rve"),
            P("macro", "rve"),
            P("macro", "rve", None, None, None),
            P("macro", "rve", None),
            P("macro", "rve", None),
            P("macro", None, "rve"),
            P("macro", None, "rve"),
        ),
        out_specs=(P(None, "macro"), P("macro", "rve", None)),
        check_vma=False,
    )
```

```python
import functools

import jax
import jax.numpy as jnp
from jax import lax
from jax.experimental import pallas as pl
from jax.experimental.pallas import tpu as pltpu
from jax.sharding import PartitionSpec as P

EPSILON = 1e-06
MESH = pl.DeviceIdType.MESH
HIGHEST = lax.Precision.HIGHEST
F32 = jnp.float32
BF16 = jnp.bfloat16
LANES = 128
NT = (((1,), (1,)), ((), ()))


def split(values):
    high = values.astype(BF16)
    return high, (values - high.astype(F32)).astype(BF16)


def dot(left, right):
    return jnp.dot(left, right, preferred_element_type=F32)


def dot_nt(left, right, precision=None):
    return lax.dot_general(left, right, NT, precision=precision, preferred_element_type=F32)


def apply_split(high, low, values):
    value_high, value_low = split(values)
    width = values.shape[1]
    wide = dot(high, jnp.concatenate([value_high, value_low], axis=1))
    return wide[:, :width] + wide[:, width:] + dot(low, value_high)


def apply_rows(values, high, low):
    value_high, value_low = split(values)
    rows = values.shape[0]
    tall = dot(jnp.concatenate([value_high, value_low], axis=0), high)
    return tall[:rows] + tall[rows:] + dot(value_high, low)


def square_nt(values):
    high, low = split(values)
    return dot_nt(high, high) + (dot_nt(high, low) + dot_nt(low, high))


def iota(shape, dim):
    return lax.broadcasted_iota(jnp.int32, shape, dim)


def pad_rows(values, rows):
    missing = rows - values.shape[0]
    if missing == 0:
        return values
    return jnp.concatenate([values, jnp.zeros((missing, values.shape[1]), values.dtype)], axis=0)


def col_sum(values):
    return jnp.sum(values, axis=0, keepdims=True)


def kernel(
    groups, parts, capacity,
    deform_hbm, plastic_hbm, route_hbm, stiff_hbm, cubic_hbm, coupling_hbm, conn_ref,
    iface_hbm, load_hbm, average_hbm,
    stress_ref, field_ref,
    deform_ref, plastic_ref, route_ref, stiff_ref, cubic_ref, coupling_ref,
    iface_ref, load_ref, average_ref,
    whole, stiff_high, stiff_low,
    out_points, in_points, edge_out, edge_in,
    halo_out, halo_in, gram_buf, first_buf, mean_buf, second_buf, out_rows, in_rows, field_buf,
    input_sem, output_sem,
    point_send, point_recv, edge_send, edge_recv, halo_send, halo_recv,
    gram_send, gram_recv, first_send, first_recv, mean_send, mean_recv, second_send, second_recv, row_send, row_recv,
):
    group = lax.axis_index("macro")
    part = lax.axis_index("rve")
    blocks, slots, block = coupling_ref.shape[1], coupling_ref.shape[2], coupling_ref.shape[3]
    dofs = blocks * block
    comps, points = deform_ref.shape
    padded = out_points.shape[1]
    columns = groups * capacity
    places = groups * padded

    barrier = pltpu.get_barrier_semaphore()
    for step in range(1, parts):
        pl.semaphore_signal(
            barrier, inc=1, device_id={"rve": lax.rem(part + step, parts)}, device_id_type=MESH
        )
    for step in range(1, groups):
        pl.semaphore_signal(
            barrier, inc=1, device_id={"macro": lax.rem(group + step, groups)}, device_id_type=MESH
        )

    loads = []
    for source, target in (
        (coupling_hbm, coupling_ref), (iface_hbm, iface_ref), (load_hbm, load_ref),
        (cubic_hbm, cubic_ref), (stiff_hbm, stiff_ref), (deform_hbm, deform_ref),
        (plastic_hbm, plastic_ref), (route_hbm, route_ref), (average_hbm, average_ref),
    ):
        loads.append(pltpu.make_async_copy(source, target, input_sem.at[len(loads)]))
        loads[-1].start()
    coupling_load, iface_load = loads[:2]
    early_loads, late_loads = loads[2:5], loads[5:]

    def exchange(source, target, send, recv):
        copies = []
        for step in range(1, groups):
            peer = lax.rem(group + step, groups)
            copies.append(pltpu.make_async_remote_copy(
                src_ref=source.at[peer], dst_ref=target.at[group],
                send_sem=send.at[step - 1], recv_sem=recv.at[step - 1],
                device_id={"macro": peer}, device_id_type=MESH,
            ))
            copies[-1].start()
        return copies

    def share(buffer, send, recv):
        copies = []
        for step in range(1, parts):
            copies.append(pltpu.make_async_remote_copy(
                src_ref=buffer.at[part], dst_ref=buffer.at[part],
                send_sem=send.at[step - 1], recv_sem=recv.at[step - 1],
                device_id={"rve": lax.rem(part + step, parts)}, device_id_type=MESH,
            ))
            copies[-1].start()
        return copies

    after, behind = lax.rem(part + 1, parts), lax.rem(part + parts - 1, parts)

    def to_neighbours(first, last, target, send, recv):
        copies = []
        for place, (source, peer) in enumerate(((last, after), (first, behind))):
            copies.append(pltpu.make_async_remote_copy(
                src_ref=source, dst_ref=target.at[place],
                send_sem=send.at[place], recv_sem=recv.at[place],
                device_id={"rve": peer}, device_id_type=MESH,
            ))
            copies[-1].start()
        return copies

    def arrive(copies):
        for copy in copies:
            copy.wait_recv()

    def gathered(buffer):
        total = buffer[0]
        for other in range(1, parts):
            total = total + buffer[other]
        return total

    coupling_load.wait()
    lane = iota((block, LANES), 1) < block
    doubled = []
    for row in range(blocks):
        square = square_nt(coupling_ref[0, row].reshape(slots * block, block))
        doubled.append([])
        for slot in range(slots):
            spring = square[slot * block:(slot + 1) * block, slot * block:(slot + 1) * block]
            doubled[row].append(jnp.concatenate([spring, spring], axis=1))

    def mark(row, slot, far):
        if row == far:
            return jnp.float32(0.0)
        return jnp.where(conn_ref[0, slot, row] == far, 1.0, 0.0).astype(F32)

    for row in range(blocks):
        own = doubled[row][0]
        for slot in range(1, slots):
            own = own + doubled[row][slot]
        for other in range(blocks):
            if other != row:
                for slot in range(slots):
                    own = own + doubled[other][slot] * mark(other, slot, row)
        for pair in range(blocks // 2):
            left, right = 2 * pair, 2 * pair + 1
            value = jnp.zeros((block, LANES), F32)
            for slot in range(slots):
                value = value - doubled[row][slot] * jnp.where(
                    lane, mark(row, slot, left), mark(row, slot, right)
                )
                value = value - jnp.where(
                    lane, doubled[left][slot] * mark(left, slot, row),
                    doubled[right][slot] * mark(right, slot, row),
                )
            if row == left:
                value = value + jnp.where(lane, own, 0.0)
            if row == right:
                value = value + jnp.where(lane, 0.0, own)
            whole[row * block:(row + 1) * block, pair * LANES:(pair + 1) * LANES] = value

    iface_load.wait()
    for copy in early_loads:
        copy.wait()
    own_edge = iface_ref[0]
    own_spring = square_nt(own_edge)
    own_high, own_low = split(own_spring)
    diagonal = iota((dofs, dofs), 0) == iota((dofs, dofs), 1)
    stiffness = whole[...] + jnp.where(diagonal, stiff_ref[...], 0.0)
    high, low = split(stiffness)
    stiff_high[...] = high
    stiff_low[...] = low
    high, low = split(stiffness[:block, :block] + own_spring)
    stiff_high[:block, :block] = high
    stiff_low[:block, :block] = low

    maps = pad_rows(load_ref[:, 0, :], 16)
    cubic = pad_rows(cubic_ref[...], 16)

    def ends(values):
        return jnp.concatenate([values[:, :block], values[:, dofs - block:]], axis=1)

    image_map = apply_rows(maps, stiff_high[...], stiff_low[...])
    packed_rows = edge_out.shape[0] - block // 2
    edge_out[:packed_rows, :] = pad_rows(
        ends(jnp.concatenate([maps[:comps], image_map[:comps], cubic[:1]], axis=0)), packed_rows
    )
    edge_out[packed_rows:, :] = jnp.concatenate([own_edge[:block // 2], own_edge[block // 2:]], axis=1)

    pl.semaphore_wait(barrier, groups + parts - 2)

    sends = []
    edge_copies = to_neighbours(edge_out, edge_out, edge_in, edge_send, edge_recv)

    for copy in late_loads:
        copy.wait()
    route = route_ref[...]
    hot = (iota((groups, points), 0) == route).astype(F32)
    before = (iota((points, points), 0) < iota((points, points), 1)).astype(BF16)
    rank = col_sum(hot * dot(hot.astype(BF16), before))
    slot_of = (route * padded).astype(F32) + rank
    select = (iota((places, points), 0).astype(F32) == slot_of).astype(F32)
    sent = pad_rows(
        jnp.concatenate([deform_ref[...], plastic_ref[...].astype(F32)], axis=0), LANES
    )
    outgoing = dot_nt(select, sent, HIGHEST)
    out_points[...] = outgoing.reshape(groups, padded, LANES)
    point_copies = exchange(out_points, in_points, point_send, point_recv)
    sends += point_copies + edge_copies
    in_points[group] = out_points[group]
    average_high, average_low = split(pad_rows(average_ref[:, 0, :], 16))

    arrive(edge_copies)
    packed = edge_in[1, packed_rows:, :]
    next_spring = square_nt(jnp.concatenate([packed[:, :block], packed[:, block:]], axis=0))
    next_high, next_low = split(next_spring)
    high, low = split(stiffness[dofs - block:, dofs - block:] + next_spring)
    stiff_high[dofs - block:, dofs - block:] = high
    stiff_low[dofs - block:, dofs - block:] = low

    def own_rows(values):
        return apply_rows(values, own_high, own_low)

    def next_rows(values):
        return apply_rows(values, next_high, next_low)

    def unpack(values):
        return jnp.concatenate([
            pad_rows(values[:comps], 16), pad_rows(values[comps:2 * comps], 16),
            pad_rows(values[2 * comps:2 * comps + 1], 16),
        ], axis=0)

    prev_edge, next_edge = unpack(edge_in[0, :packed_rows]), unpack(edge_in[1, :packed_rows])
    prev_map, next_map = prev_edge[0:16, block:], next_edge[0:16, :block]
    first_map, last_map = maps[:, :block], maps[:, dofs - block:]
    through_own = own_rows(jnp.concatenate([prev_map, first_map], axis=0))
    through_next = next_rows(jnp.concatenate([next_map, last_map], axis=0))
    prev_image = prev_edge[16:32, block:] + through_own[:16] - through_own[16:]
    next_image = next_edge[16:32, :block] - through_next[16:]
    image_map = jnp.concatenate([
        image_map[:, :block] - through_own[:16],
        image_map[:, block:dofs - block],
        image_map[:, dofs - block:] + through_next[16:] - through_next[:16],
    ], axis=1)
    second_map = apply_rows(image_map, stiff_high[...], stiff_low[...])
    second_map = jnp.concatenate([
        second_map[:, :block] - own_rows(prev_image),
        second_map[:, block:dofs - block],
        second_map[:, dofs - block:] - next_rows(next_image),
    ], axis=1)
    basis = jnp.concatenate([maps, image_map, second_map, cubic], axis=0)
    products = dot_nt(basis[0:32], basis[0:48], HIGHEST)
    gram_buf[part, 0:16] = jnp.concatenate(
        [products[0:16, 0:32], products[16:32, 16:48], jnp.zeros((16, LANES - 64), F32)], axis=1
    )
    gram_buf[part, 16:32] = ends(second_map)
    gram_copies = share(gram_buf, gram_send, gram_recv)
    sends += gram_copies

    basis_cols = jnp.transpose(basis)
    arrive(point_copies)

    def compact(rows):
        rows = rows.reshape(places, LANES)
        if padded == capacity:
            return rows
        row, col = iota((columns, places), 0), iota((columns, places), 1)
        take = (col == (row // capacity) * padded + row % capacity).astype(F32)
        return jnp.dot(take, rows, precision=HIGHEST, preferred_element_type=F32)

    received = jnp.transpose(compact(in_points[...]))[:16]
    flag = received[comps:comps + 1]
    strain = jnp.where(iota((16, columns), 0) < comps, received, 0.0)
    hard = basis_cols[:, 48:49] * flag

    arrive(gram_copies)
    ghost_basis = jnp.concatenate([
        jnp.concatenate([prev_map, next_map], axis=1),
        jnp.concatenate([prev_image, next_image], axis=1),
        jnp.concatenate(
            [gram_buf[behind, 16:32][:, block:], gram_buf[after, 16:32][:, :block]], axis=1
        ),
        jnp.concatenate([prev_edge[32:48, block:], next_edge[32:48, :block]], axis=1),
    ], axis=0)
    ghost_cols = jnp.transpose(ghost_basis)
    ghost_hard = ghost_cols[:, 48:49] * flag
    gram = gathered(gram_buf)
    forms = jnp.concatenate(
        [gram[0:16, 0:16], gram[0:16, 16:32], gram[0:16, 32:48], gram[0:16, 48:64]], axis=0
    )
    forms = jnp.dot(forms, strain, precision=HIGHEST, preferred_element_type=F32)
    norm = col_sum(forms[0:16] * strain)
    curve = col_sum(forms[16:32] * strain)
    third = col_sum(forms[32:48] * strain)
    fourth = col_sum(forms[48:64] * strain)

    def second_step(norm, curve, left_norm, left_curve, cross):
        ratio = left_norm / (norm + EPSILON)
        next_curve = left_curve + ratio * (2.0 * cross + ratio * curve)
        next_curve = jnp.maximum(next_curve, 0.09 * left_norm)
        next_len = left_norm / (next_curve + EPSILON)
        return next_len, next_len * ratio

    step_len = norm / (curve + EPSILON)
    left_norm = jnp.maximum(norm - step_len * (2.0 * curve - step_len * third), 0.0)
    left_curve = curve - step_len * (2.0 * third - step_len * fourth)
    cross = curve - step_len * third
    next_len, carried = second_step(norm, curve, left_norm, left_curve, cross)
    along = step_len + carried + next_len
    across = next_len * step_len
    zero = jnp.zeros_like(strain)
    weights = jnp.concatenate([
        jnp.concatenate([along * strain, -across * strain, zero], axis=0),
        jnp.concatenate([strain, -along * strain, across * strain], axis=0),
    ], axis=1)
    both = jnp.dot(
        jnp.concatenate([basis_cols[:, :48], ghost_cols[:, :48]], axis=0), weights,
        precision=HIGHEST, preferred_element_type=F32,
    )
    solved = both[:dofs, :columns]
    hard_square = hard * solved * solved
    tangent = 3.0 * hard_square
    residue = both[:dofs, columns:] - hard_square * solved
    ghost_solved = both[dofs:, :columns]
    ghost = both[dofs:, columns:] - ghost_hard * ghost_solved * ghost_solved * ghost_solved

    def coupled(product, ghost):
        top = product[:block] - apply_split(own_high, own_low, ghost[:block])
        bottom = product[dofs - block:] - apply_split(next_high, next_low, ghost[block:])
        return jnp.concatenate([top, product[block:dofs - block], bottom], axis=0)

    def averaged(values):
        return apply_split(average_high, average_low, values)[:comps]

    image = coupled(apply_split(stiff_high[...], stiff_low[...], residue), ghost)
    image = image + tangent * residue
    first_buf[part] = pad_rows(jnp.concatenate([
        col_sum(residue * residue), col_sum(residue * image),
    ], axis=0), first_buf.shape[1])
    first_copies = share(first_buf, first_send, first_recv)
    halo_out[0] = image[:block]
    halo_out[1] = image[dofs - block:]
    halo_copies = to_neighbours(
        halo_out.at[0], halo_out.at[1], halo_in, halo_send, halo_recv
    )
    second = apply_split(stiff_high[...], stiff_low[...], image)
    mean_buf[part] = pad_rows(jnp.concatenate(
        [averaged(solved), averaged(residue), averaged(image)], axis=0
    ), mean_buf.shape[1])
    mean_copies = share(mean_buf, mean_send, mean_recv)
    sends += halo_copies + first_copies + mean_copies
    arrive(first_copies)
    sums = gathered(first_buf)
    norm, curve = sums[0:1], sums[1:2]
    step_len = norm / (curve + EPSILON)
    left = residue - step_len * image
    arrive(halo_copies)
    second = coupled(second, halo_in[...].reshape(2 * block, columns)) + tangent * image
    left_image = image - step_len * second
    second_buf[part] = pad_rows(jnp.concatenate(
        [col_sum(left * left), col_sum(left * left_image), col_sum(left * image)], axis=0
    ), 8)
    second_copies = share(second_buf, second_send, second_recv)
    sends += second_copies
    arrive(mean_copies)
    means = gathered(mean_buf)
    arrive(second_copies)
    last = gathered(second_buf)
    next_len, carried = second_step(norm, curve, last[0:1], last[1:2], last[2:3])
    along = step_len + carried
    total = (
        means[:comps] + along * means[comps:2 * comps]
        + next_len * (means[comps:2 * comps] - step_len * means[2 * comps:3 * comps])
    )

    rows = jnp.transpose(pad_rows(total, LANES))
    if padded != capacity:
        row, col = iota((places, columns), 0), iota((places, columns), 1)
        spread = jnp.logical_and(
            col == (row // padded) * capacity + row % padded, row % padded < capacity
        ).astype(F32)
        rows = jnp.dot(spread, rows, precision=HIGHEST, preferred_element_type=F32)
    out_rows[...] = rows.reshape(groups, padded, LANES)
    row_copies = exchange(out_rows, in_rows, row_send, row_recv)
    sends += row_copies
    in_rows[group] = out_rows[group]
    field_buf[0] = solved + along * residue + next_len * left
    field_ref[...] = field_buf[...]
    arrive(row_copies)
    back = jnp.transpose(in_rows[...].reshape(places, LANES))[:16]
    picked = jnp.dot(back, select, precision=HIGHEST, preferred_element_type=F32)
    stress_ref[...] = picked[:comps]
    for copy in sends:
        copy.wait_send()


def place(stress_ref, field_ref, stress_out, field_out, sem):
    first = pltpu.make_async_copy(field_ref, field_out, sem.at[0])
    second = pltpu.make_async_copy(stress_ref, stress_out, sem.at[1])
    first.start()
    second.start()
    first.wait()
    second.wait()


def solution(mesh):
    groups, parts = mesh.shape["macro"], mesh.shape["rve"]

    def shards(deform, plastic, route, stiff, cubic, coupling, conn, iface, load_map, average_map):
        comps, points = deform.shape
        blocks, block = coupling.shape[1], coupling.shape[3]
        dofs = blocks * block
        capacity = 2 * points // groups
        columns = groups * capacity
        padded = -(-capacity // 8) * 8
        edge_rows = -(-(2 * comps + 1) // 8) * 8
        vmem = pl.BlockSpec(memory_space=pltpu.VMEM)
        hbm = pl.BlockSpec(memory_space=pltpu.HBM)
        dma = pltpu.SemaphoreType.DMA
        stress, field = pl.pallas_call(
            functools.partial(kernel, groups, parts, capacity),
            out_shape=(
                pltpu.VMEM((comps, points), F32),
                pltpu.VMEM((1, dofs, columns), F32),
            ),
            in_specs=[hbm] * 6 + [pl.BlockSpec(memory_space=pltpu.SMEM)] + [hbm] * 3,
            out_specs=(vmem, vmem),
            scratch_shapes=[
                pltpu.VMEM(deform.shape, F32),
                pltpu.VMEM((1, points), jnp.int32),
                pltpu.VMEM((1, points), jnp.int32),
                pltpu.VMEM((1, dofs), F32),
                pltpu.VMEM((1, dofs), F32),
                pltpu.VMEM(coupling.shape, F32),
                pltpu.VMEM(iface.shape, F32),
                pltpu.VMEM((comps, 1, dofs), F32),
                pltpu.VMEM((comps, 1, dofs), F32),
                pltpu.VMEM((dofs, dofs), F32),
                pltpu.VMEM((dofs, dofs), BF16),
                pltpu.VMEM((dofs, dofs), BF16),
                pltpu.VMEM((groups, padded, LANES), F32),
                pltpu.VMEM((groups, padded, LANES), F32),
                pltpu.VMEM((edge_rows + block // 2, LANES), F32),
                pltpu.VMEM((2, edge_rows + block // 2, LANES), F32),
                pltpu.VMEM((2, block, columns), F32),
                pltpu.VMEM((2, block, columns), F32),
                pltpu.VMEM((parts, 32, LANES), F32),
                pltpu.VMEM((parts, 8, columns), F32),
                pltpu.VMEM((parts, 32, columns), F32),
                pltpu.VMEM((parts, 8, columns), F32),
                pltpu.VMEM((groups, padded, LANES), F32),
                pltpu.VMEM((groups, padded, LANES), F32),
                pltpu.VMEM((1, dofs, columns), F32),
                dma((9,)), dma,
                dma((groups - 1,)), dma((groups - 1,)),
                dma((2,)), dma((2,)),
                dma((2,)), dma((2,)),
                dma((parts - 1,)), dma((parts - 1,)),
                dma((parts - 1,)), dma((parts - 1,)),
                dma((parts - 1,)), dma((parts - 1,)),
                dma((parts - 1,)), dma((parts - 1,)),
                dma((groups - 1,)), dma((groups - 1,)),
            ],
            compiler_params=pltpu.CompilerParams(
                collective_id=0, has_side_effects=True, vmem_limit_bytes=60 * 1024 * 1024
            ),
        )(
            deform, plastic[None], route[None], stiff, cubic, coupling,
            jnp.transpose(conn, (0, 2, 1)), iface,
            jnp.transpose(load_map, (1, 0, 2)), jnp.transpose(average_map, (1, 0, 2)),
        )
        return pl.pallas_call(
            place,
            out_shape=(
                jax.ShapeDtypeStruct((comps, points), F32),
                jax.ShapeDtypeStruct((1, dofs, columns), F32),
            ),
            in_specs=[vmem, vmem], out_specs=(hbm, hbm),
            scratch_shapes=[dma((2,))],
        )(*(pltpu.with_memory_space_constraint(x, pltpu.VMEM) for x in (stress, field)))

    return jax.shard_map(
        shards,
        mesh=mesh,
        in_specs=(
            P(None, "macro"),
            P("macro"),
            P("macro"),
            P("macro", "rve"),
            P("macro", "rve"),
            P("macro", "rve", None, None, None),
            P("macro", "rve", None),
            P("macro", "rve", None),
            P("macro", None, "rve"),
            P("macro", None, "rve"),
        ),
        out_specs=(P(None, "macro"), P("macro", "rve", None)),
        check_vma=False,
    )
```

```python
import functools

import jax
import jax.numpy as jnp
from jax import lax
from jax.experimental import pallas as pl
from jax.experimental.pallas import tpu as pltpu
from jax.sharding import PartitionSpec as P

EPSILON = 1e-06
SCALE = 2.0 ** -20
MESH = pl.DeviceIdType.MESH
HIGHEST = lax.Precision.HIGHEST
F32 = jnp.float32
BF16 = jnp.bfloat16
LANES = 128
NT = (((1,), (1,)), ((), ()))


def split(values):
    high = values.astype(BF16)
    return high, (values - high.astype(F32)).astype(BF16)


def dot(left, right):
    return jnp.dot(left, right, preferred_element_type=F32)


def dot_nt(left, right, precision=None):
    return lax.dot_general(left, right, NT, precision=precision, preferred_element_type=F32)


def apply_split(high, low, values):
    value_high, value_low = split(values)
    width = values.shape[1]
    wide = dot(high, jnp.concatenate([value_high, value_low], axis=1))
    return wide[:, :width] + wide[:, width:] + dot(low, value_high)


def apply_rows(values, high, low):
    value_high, value_low = split(values)
    rows = values.shape[0]
    tall = dot(jnp.concatenate([value_high, value_low], axis=0), high)
    return tall[:rows] + tall[rows:] + dot(value_high, low)


def square_nt(values):
    high, low = split(values)
    return dot_nt(high, high) + (dot_nt(high, low) + dot_nt(low, high))


def iota(shape, dim):
    return lax.broadcasted_iota(jnp.int32, shape, dim)


def pad_rows(values, rows):
    missing = rows - values.shape[0]
    if missing == 0:
        return values
    return jnp.concatenate([values, jnp.zeros((missing, values.shape[1]), values.dtype)], axis=0)


def col_sum(values):
    return jnp.sum(values, axis=0, keepdims=True)


def kernel(
    groups, parts, capacity,
    deform_hbm, plastic_hbm, route_hbm, stiff_hbm, cubic_hbm, coupling_hbm, conn_ref,
    iface_hbm, load_hbm, average_hbm,
    stress_ref, field_ref,
    deform_ref, plastic_ref, route_ref, stiff_ref, cubic_ref, coupling_ref,
    iface_ref, load_ref, average_ref,
    whole, stiff_high, stiff_low,
    out_points, in_points, edge_out, edge_in,
    base_out, base_in, last_in, map_out, map_in, head_out, head_in,
    gram_buf, sum_buf, out_rows, in_rows,
    input_sem,
    point_send, point_recv, edge_send, edge_recv, ghost_send, ghost_recv,
    gram_send, gram_recv, sum_send, sum_recv, row_send, row_recv,
):
    group = lax.axis_index("macro")
    part = lax.axis_index("rve")
    blocks, slots, block = coupling_ref.shape[1], coupling_ref.shape[2], coupling_ref.shape[3]
    dofs = blocks * block
    comps, points = deform_ref.shape
    padded = out_points.shape[1]
    columns = groups * capacity
    places = groups * padded

    barrier = pltpu.get_barrier_semaphore()
    for step in range(1, parts):
        pl.semaphore_signal(
            barrier, inc=1, device_id={"rve": lax.rem(part + step, parts)}, device_id_type=MESH
        )
    for step in range(1, groups):
        pl.semaphore_signal(
            barrier, inc=1, device_id={"macro": lax.rem(group + step, groups)}, device_id_type=MESH
        )

    loads = []
    for source, target in (
        (coupling_hbm, coupling_ref), (iface_hbm, iface_ref), (load_hbm, load_ref),
        (cubic_hbm, cubic_ref), (stiff_hbm, stiff_ref), (deform_hbm, deform_ref),
        (plastic_hbm, plastic_ref), (route_hbm, route_ref), (average_hbm, average_ref),
    ):
        loads.append(pltpu.make_async_copy(source, target, input_sem.at[len(loads)]))
        loads[-1].start()
    coupling_load, iface_load = loads[:2]
    early_loads, late_loads = loads[2:5], loads[5:]

    def exchange(source, target, send, recv):
        copies = []
        for step in range(1, groups):
            peer = lax.rem(group + step, groups)
            copies.append(pltpu.make_async_remote_copy(
                src_ref=source.at[peer], dst_ref=target.at[group],
                send_sem=send.at[step - 1], recv_sem=recv.at[step - 1],
                device_id={"macro": peer}, device_id_type=MESH,
            ))
            copies[-1].start()
        return copies

    def share(buffer, send, recv):
        copies = []
        for step in range(1, parts):
            copies.append(pltpu.make_async_remote_copy(
                src_ref=buffer.at[part], dst_ref=buffer.at[part],
                send_sem=send.at[step - 1], recv_sem=recv.at[step - 1],
                device_id={"rve": lax.rem(part + step, parts)}, device_id_type=MESH,
            ))
            copies[-1].start()
        return copies

    after, behind = lax.rem(part + 1, parts), lax.rem(part + parts - 1, parts)

    def push(source, target, peer, send, recv, place):
        copy = pltpu.make_async_remote_copy(
            src_ref=source, dst_ref=target, send_sem=send.at[place], recv_sem=recv.at[place],
            device_id={"rve": peer}, device_id_type=MESH,
        )
        copy.start()
        return copy

    def arrive(copies):
        for copy in copies:
            copy.wait_recv()

    def gathered(buffer):
        total = buffer[0]
        for other in range(1, parts):
            total = total + buffer[other]
        return total

    coupling_load.wait()
    lane = iota((block, LANES), 1) < block
    doubled = []
    for row in range(blocks):
        square = square_nt(coupling_ref[0, row].reshape(slots * block, block))
        doubled.append([])
        for slot in range(slots):
            spring = square[slot * block:(slot + 1) * block, slot * block:(slot + 1) * block]
            doubled[row].append(jnp.concatenate([spring, spring], axis=1))

    def mark(row, slot, far):
        if row == far:
            return jnp.float32(0.0)
        return jnp.where(conn_ref[0, slot, row] == far, 1.0, 0.0).astype(F32)

    for row in range(blocks):
        own = doubled[row][0]
        for slot in range(1, slots):
            own = own + doubled[row][slot]
        for other in range(blocks):
            if other != row:
                for slot in range(slots):
                    own = own + doubled[other][slot] * mark(other, slot, row)
        for pair in range(blocks // 2):
            left, right = 2 * pair, 2 * pair + 1
            value = jnp.zeros((block, LANES), F32)
            for slot in range(slots):
                value = value - doubled[row][slot] * jnp.where(
                    lane, mark(row, slot, left), mark(row, slot, right)
                )
                value = value - jnp.where(
                    lane, doubled[left][slot] * mark(left, slot, row),
                    doubled[right][slot] * mark(right, slot, row),
                )
            if row == left:
                value = value + jnp.where(lane, own, 0.0)
            if row == right:
                value = value + jnp.where(lane, 0.0, own)
            whole[row * block:(row + 1) * block, pair * LANES:(pair + 1) * LANES] = value

    iface_load.wait()
    for copy in early_loads:
        copy.wait()
    own_edge = iface_ref[0]
    own_spring = square_nt(own_edge)
    own_high, own_low = split(own_spring)
    diagonal = iota((dofs, dofs), 0) == iota((dofs, dofs), 1)
    stiffness = whole[...] + jnp.where(diagonal, stiff_ref[...], 0.0)
    high, low = split(stiffness)
    stiff_high[:dofs, :] = high
    stiff_low[:dofs, :] = low
    whole[dofs - block:, :] = stiffness[dofs - block:, :]
    high, low = split(stiffness[:block, :block] + own_spring)
    stiff_high[:block, :block] = high
    stiff_low[:block, :block] = low

    maps = pad_rows(load_ref[:, 0, :], 16)
    cubic = pad_rows(cubic_ref[...], 16)

    def ends(values):
        return jnp.concatenate([values[:, :block], values[:, dofs - block:]], axis=1)

    image_map = apply_rows(maps, stiff_high[:dofs, :], stiff_low[:dofs, :])
    packed_rows = base_out.shape[0]
    packed = pad_rows(jnp.concatenate([maps[:comps], image_map[:comps], cubic[:1]], axis=0), packed_rows)
    base_out[...] = packed
    edge_out[:packed_rows, :] = ends(packed)
    edge_out[packed_rows:, :] = jnp.concatenate([own_edge[:block // 2], own_edge[block // 2:]], axis=1)

    pl.semaphore_wait(barrier, groups + parts - 2)

    sends = []
    edge_copies = [
        push(edge_out, edge_in.at[0], after, edge_send, edge_recv, 0),
        push(edge_out, edge_in.at[1], behind, edge_send, edge_recv, 1),
    ]

    for copy in late_loads:
        copy.wait()
    route = route_ref[...]
    hot = (iota((groups, points), 0) == route).astype(F32)
    before = (iota((points, points), 0) < iota((points, points), 1)).astype(BF16)
    rank = col_sum(hot * dot(hot.astype(BF16), before))
    slot_of = (route * padded).astype(F32) + rank
    select = (iota((places, points), 0).astype(F32) == slot_of).astype(F32)
    sent = pad_rows(
        jnp.concatenate([deform_ref[...], plastic_ref[...].astype(F32)], axis=0), LANES
    )
    outgoing = dot_nt(select, sent, HIGHEST)
    out_points[...] = outgoing.reshape(groups, padded, LANES)
    point_copies = exchange(out_points, in_points, point_send, point_recv)
    ghost_copies = [
        push(base_out, base_in, after, ghost_send, ghost_recv, 0),
        push(whole.at[pl.ds(dofs - block, block)], last_in, after, ghost_send, ghost_recv, 1),
    ]
    sends += point_copies + edge_copies + ghost_copies
    in_points[group] = out_points[group]
    average_high, average_low = split(pad_rows(average_ref[:, 0, :], 16))
    stiff_high[dofs:, :] = average_high
    stiff_low[dofs:, :] = average_low

    arrive(edge_copies)
    packed = edge_in[1, packed_rows:, :]
    next_spring = square_nt(jnp.concatenate([packed[:, :block], packed[:, block:]], axis=0))
    next_high, next_low = split(next_spring)
    high, low = split(stiffness[dofs - block:, dofs - block:] + next_spring)
    stiff_high[dofs - block:dofs, dofs - block:] = high
    stiff_low[dofs - block:dofs, dofs - block:] = low

    def own_rows(values):
        return apply_rows(values, own_high, own_low)

    def next_rows(values):
        return apply_rows(values, next_high, next_low)

    def unpack(values):
        return jnp.concatenate([
            pad_rows(values[:comps], 16), pad_rows(values[comps:2 * comps], 16),
            pad_rows(values[2 * comps:2 * comps + 1], 16),
        ], axis=0)

    prev_edge, next_edge = unpack(edge_in[0, :packed_rows]), unpack(edge_in[1, :packed_rows])
    prev_map, next_map = prev_edge[0:16, block:], next_edge[0:16, :block]
    first_map, last_map = maps[:, :block], maps[:, dofs - block:]
    through_own = own_rows(jnp.concatenate([prev_map, first_map], axis=0))
    through_next = next_rows(jnp.concatenate([next_map, last_map], axis=0))
    prev_image = prev_edge[16:32, block:] + through_own[:16] - through_own[16:]
    next_image = next_edge[16:32, :block] - through_next[16:]
    image_map = jnp.concatenate([
        image_map[:, :block] - through_own[:16],
        image_map[:, block:dofs - block],
        image_map[:, dofs - block:] + through_next[16:] - through_next[:16],
    ], axis=1)
    second_map = apply_rows(image_map, stiff_high[:dofs, :], stiff_low[:dofs, :])
    second_map = jnp.concatenate([
        second_map[:, :block] - own_rows(prev_image),
        second_map[:, block:dofs - block],
        second_map[:, dofs - block:] - next_rows(next_image),
    ], axis=1)
    basis = jnp.concatenate([maps, image_map, second_map, cubic], axis=0)
    products = dot_nt(basis[0:32], basis[0:48], HIGHEST)
    gram_buf[part] = jnp.concatenate([
        products[0:16, 0:32], products[16:32, 16:48], image_map[:, :block],
    ], axis=1)
    map_out[...] = second_map
    head_out[...] = second_map[:, :LANES]
    map_copies = [
        push(map_out, map_in, after, ghost_send, ghost_recv, 2),
        push(head_out, head_in, behind, ghost_send, ghost_recv, 3),
    ]
    gram_copies = share(gram_buf, gram_send, gram_recv)
    sends += map_copies + gram_copies

    basis_cols = jnp.transpose(basis)
    arrive(point_copies)

    def compact(rows):
        rows = rows.reshape(places, LANES)
        if padded == capacity:
            return rows
        row, col = iota((columns, places), 0), iota((columns, places), 1)
        take = (col == (row // capacity) * padded + row % capacity).astype(F32)
        return jnp.dot(take, rows, precision=HIGHEST, preferred_element_type=F32)

    received = jnp.transpose(compact(in_points[...]))[:16]
    flag = received[comps:comps + 1]
    strain = jnp.where(iota((16, columns), 0) < comps, received, 0.0)
    hard = basis_cols[:, 48:49] * flag

    arrive(ghost_copies)
    prev_rows = unpack(base_in[...])
    last_rows = last_in[...]
    last_high, last_low = split(jnp.concatenate(
        [last_rows[:, :dofs - LANES], last_rows[:, dofs - LANES:] + jnp.concatenate([jnp.zeros_like(own_spring), own_spring], axis=1)],
        axis=1,
    ))

    arrive(gram_copies + map_copies)
    prev_basis = jnp.concatenate([
        prev_rows[0:16],
        jnp.concatenate([
            gram_buf[behind][:, block:], prev_rows[16:32, block:dofs - block], prev_image,
        ], axis=1),
        map_in[...],
        prev_rows[32:48],
    ], axis=0)
    next_basis = jnp.concatenate([
        next_map, next_image, head_in[...][:, :block], next_edge[32:48, :block],
    ], axis=0)
    ghost_basis = jnp.concatenate([prev_basis, next_basis], axis=1)
    ghost_cols = jnp.transpose(ghost_basis)
    ghost_hard = ghost_cols[:, 48:49] * flag
    gram = gathered(gram_buf)
    forms = jnp.concatenate(
        [gram[0:16, 0:16], gram[0:16, 16:32], gram[0:16, 32:48], gram[0:16, 48:64]], axis=0
    )
    forms = jnp.dot(forms, strain, precision=HIGHEST, preferred_element_type=F32)
    norm = col_sum(forms[0:16] * strain)
    curve = col_sum(forms[16:32] * strain)
    third = col_sum(forms[32:48] * strain)
    fourth = col_sum(forms[48:64] * strain)

    def second_step(norm, curve, left_norm, left_curve, cross):
        ratio = left_norm / (norm + EPSILON)
        next_curve = left_curve + ratio * (2.0 * cross + ratio * curve)
        next_curve = jnp.maximum(next_curve, 0.09 * left_norm)
        next_len = left_norm / (next_curve + EPSILON)
        return next_len, next_len * ratio

    step_len = norm / (curve + EPSILON)
    left_norm = jnp.maximum(norm - step_len * (2.0 * curve - step_len * third), 0.0)
    left_curve = curve - step_len * (2.0 * third - step_len * fourth)
    cross = curve - step_len * third
    next_len, carried = second_step(norm, curve, left_norm, left_curve, cross)
    along = step_len + carried + next_len
    across = next_len * step_len
    zero = jnp.zeros_like(strain)
    weights = jnp.concatenate([
        jnp.concatenate([along * strain, -across * strain, zero], axis=0),
        jnp.concatenate([strain, -along * strain, across * strain], axis=0),
    ], axis=1)
    both = jnp.dot(
        jnp.concatenate([basis_cols[:, :48], ghost_cols[:, :48]], axis=0), weights,
        precision=HIGHEST, preferred_element_type=F32,
    )
    solved = both[:dofs, :columns]
    hard_square = hard * solved * solved
    tangent = 3.0 * hard_square
    residue = both[:dofs, columns:] - hard_square * solved
    ghost_solved = both[dofs:, :columns]
    ghost_square = ghost_hard * ghost_solved * ghost_solved
    ghost = both[dofs:, columns:] - ghost_square * ghost_solved
    prev_residue = ghost[:dofs]
    prev_tangent = 3.0 * ghost_square[dofs - block:dofs]
    prev_last, next_first = ghost[dofs - block:dofs], ghost[dofs:]

    product = apply_split(stiff_high[...], stiff_low[...], residue)
    pair = apply_split(own_high, own_low, jnp.concatenate([prev_last, residue[:block]], axis=1))
    through_prev = pair[:, :columns]
    through_next = apply_split(next_high, next_low, next_first)
    last_product = apply_split(last_high, last_low, prev_residue)
    last_image = last_product + prev_tangent * prev_last - pair[:, columns:]
    plain = product[:dofs] + tangent * residue
    image = jnp.concatenate([
        plain[:block] - through_prev, plain[block:dofs - block], plain[dofs - block:] - through_next,
    ], axis=0)
    second = apply_split(stiff_high[...], stiff_low[...], image)
    through_last = apply_split(own_high, own_low, last_image)

    def one_sided(values, through):
        return jnp.concatenate([values[:block] - 2.0 * through, values[block:]], axis=0)

    scaled = SCALE * image
    length = jnp.sqrt(col_sum(scaled * scaled))
    inverse = jnp.where(length > 0.0, SCALE / jnp.where(length > 0.0, length, 1.0), 0.0)
    length = length * (1.0 / SCALE)
    unit = inverse * image
    along_unit = col_sum(residue * unit)
    rest = residue - along_unit * unit
    form_unit = inverse * one_sided(second[:dofs] + tangent * image, through_last)
    form_rest = one_sided(plain, through_prev) - along_unit * form_unit
    sum_buf[part] = pad_rows(jnp.concatenate([
        col_sum(residue * residue), length, along_unit, col_sum(rest * rest),
        col_sum(rest * form_rest), col_sum(rest * form_unit + unit * form_rest), col_sum(unit * form_unit),
        jnp.zeros_like(length),
        apply_split(average_high, average_low, solved)[:comps], product[dofs:dofs + comps], second[dofs:dofs + comps],
    ], axis=0), sum_buf.shape[1])
    sum_copies = share(sum_buf, sum_send, sum_recv)
    sends += sum_copies
    arrive(sum_copies)
    sums = [sum_buf[other] for other in range(parts)]
    means = sum(sums[1:], sums[0])[8:]
    norm = sum(each[0:1] for each in sums)
    curve = sum(each[1:2] * each[2:3] for each in sums)
    step_len = norm / (curve + EPSILON)
    left_norm, left_curve, cross = 0.0, 0.0, 0.0
    for each in sums:
        beyond = step_len * each[1:2] - each[2:3]
        left_norm = left_norm + (each[3:4] + beyond * beyond)
        left_curve = left_curve + (each[4:5] - beyond * (each[5:6] - beyond * each[6:7]))
        cross = cross - beyond * each[1:2]
    next_len, carried = second_step(norm, curve, left_norm, left_curve, cross)
    along = step_len + carried
    total = (
        means[:comps] + along * means[comps:2 * comps]
        + next_len * (means[comps:2 * comps] - step_len * means[2 * comps:3 * comps])
    )

    rows = jnp.transpose(pad_rows(total, LANES))
    if padded != capacity:
        row, col = iota((places, columns), 0), iota((places, columns), 1)
        spread = jnp.logical_and(
            col == (row // padded) * capacity + row % padded, row % padded < capacity
        ).astype(F32)
        rows = jnp.dot(spread, rows, precision=HIGHEST, preferred_element_type=F32)
    out_rows[...] = rows.reshape(groups, padded, LANES)
    row_copies = exchange(out_rows, in_rows, row_send, row_recv)
    sends += row_copies
    in_rows[group] = out_rows[group]
    field_ref[0] = solved + along * residue + next_len * (residue - step_len * image)
    arrive(row_copies)
    back = jnp.transpose(in_rows[...].reshape(places, LANES))[:16]
    picked = jnp.dot(back, select, precision=HIGHEST, preferred_element_type=F32)
    stress_ref[...] = picked[:comps]
    for copy in sends:
        copy.wait_send()


def place(stress_ref, field_ref, stress_out, field_out, sem):
    first = pltpu.make_async_copy(field_ref, field_out, sem.at[0])
    second = pltpu.make_async_copy(stress_ref, stress_out, sem.at[1])
    first.start()
    second.start()
    first.wait()
    second.wait()


def solution(mesh):
    groups, parts = mesh.shape["macro"], mesh.shape["rve"]

    def shards(deform, plastic, route, stiff, cubic, coupling, conn, iface, load_map, average_map):
        comps, points = deform.shape
        blocks, block = coupling.shape[1], coupling.shape[3]
        dofs = blocks * block
        capacity = 2 * points // groups
        columns = groups * capacity
        padded = -(-capacity // 8) * 8
        edge_rows = -(-(2 * comps + 1) // 8) * 8
        vmem = pl.BlockSpec(memory_space=pltpu.VMEM)
        hbm = pl.BlockSpec(memory_space=pltpu.HBM)
        dma = pltpu.SemaphoreType.DMA
        stress, field = pl.pallas_call(
            functools.partial(kernel, groups, parts, capacity),
            out_shape=(
                pltpu.VMEM((comps, points), F32),
                pltpu.VMEM((1, dofs, columns), F32),
            ),
            in_specs=[hbm] * 6 + [pl.BlockSpec(memory_space=pltpu.SMEM)] + [hbm] * 3,
            out_specs=(vmem, vmem),
            scratch_shapes=[
                pltpu.VMEM(deform.shape, F32),
                pltpu.VMEM((1, points), jnp.int32),
                pltpu.VMEM((1, points), jnp.int32),
                pltpu.VMEM((1, dofs), F32),
                pltpu.VMEM((1, dofs), F32),
                pltpu.VMEM(coupling.shape, F32),
                pltpu.VMEM(iface.shape, F32),
                pltpu.VMEM((comps, 1, dofs), F32),
                pltpu.VMEM((comps, 1, dofs), F32),
                pltpu.VMEM((dofs, dofs), F32),
                pltpu.VMEM((dofs + 16, dofs), BF16),
                pltpu.VMEM((dofs + 16, dofs), BF16),
                pltpu.VMEM((groups, padded, LANES), F32),
                pltpu.VMEM((groups, padded, LANES), F32),
                pltpu.VMEM((edge_rows + block // 2, LANES), F32),
                pltpu.VMEM((2, edge_rows + block // 2, LANES), F32),
                pltpu.VMEM((edge_rows, dofs), F32),
                pltpu.VMEM((edge_rows, dofs), F32),
                pltpu.VMEM((block, dofs), F32),
                pltpu.VMEM((16, dofs), F32),
                pltpu.VMEM((16, dofs), F32),
                pltpu.VMEM((16, LANES), F32),
                pltpu.VMEM((16, LANES), F32),
                pltpu.VMEM((parts, 16, LANES), F32),
                pltpu.VMEM((parts, -(-(8 + 3 * comps) // 8) * 8, columns), F32),
                pltpu.VMEM((groups, padded, LANES), F32),
                pltpu.VMEM((groups, padded, LANES), F32),
                dma((9,)),
                dma((groups - 1,)), dma((groups - 1,)),
                dma((2,)), dma((2,)),
                dma((4,)), dma((4,)),
                dma((parts - 1,)), dma((parts - 1,)),
                dma((parts - 1,)), dma((parts - 1,)),
                dma((groups - 1,)), dma((groups - 1,)),
            ],
            compiler_params=pltpu.CompilerParams(
                collective_id=0, has_side_effects=True, vmem_limit_bytes=60 * 1024 * 1024
            ),
        )(
            deform, plastic[None], route[None], stiff, cubic, coupling,
            jnp.transpose(conn, (0, 2, 1)), iface,
            jnp.transpose(load_map, (1, 0, 2)), jnp.transpose(average_map, (1, 0, 2)),
        )
        return pl.pallas_call(
            place,
            out_shape=(
                jax.ShapeDtypeStruct((comps, points), F32),
                jax.ShapeDtypeStruct((1, dofs, columns), F32),
            ),
            in_specs=[vmem, vmem], out_specs=(hbm, hbm),
            scratch_shapes=[dma((2,))],
        )(*(pltpu.with_memory_space_constraint(x, pltpu.VMEM) for x in (stress, field)))

    return jax.shard_map(
        shards,
        mesh=mesh,
        in_specs=(
            P(None, "macro"),
            P("macro"),
            P("macro"),
            P("macro", "rve"),
            P("macro", "rve"),
            P("macro", "rve", None, None, None),
            P("macro", "rve", None),
            P("macro", "rve", None),
            P("macro", None, "rve"),
            P("macro", None, "rve"),
        ),
        out_specs=(P(None, "macro"), P("macro", "rve", None)),
        check_vma=False,
    )
```

```python
import functools

import jax
import jax.numpy as jnp
from jax import lax
from jax.experimental import pallas as pl
from jax.experimental.pallas import tpu as pltpu
from jax.sharding import PartitionSpec as P

EPSILON = 1e-06
SCALE = 2.0 ** -20
MESH = pl.DeviceIdType.MESH
HIGHEST = lax.Precision.HIGHEST
F32 = jnp.float32
BF16 = jnp.bfloat16
LANES = 128
NT = (((1,), (1,)), ((), ()))


def split(values):
    high = values.astype(BF16)
    return high, (values - high.astype(F32)).astype(BF16)


def dot(left, right):
    return jnp.dot(left, right, preferred_element_type=F32)


def dot_nt(left, right, precision=None):
    return lax.dot_general(left, right, NT, precision=precision, preferred_element_type=F32)


def apply_split(high, low, values):
    value_high, value_low = split(values)
    width = values.shape[1]
    wide = dot(high, jnp.concatenate([value_high, value_low], axis=1))
    return wide[:, :width] + wide[:, width:] + dot(low, value_high)


def apply_rows(values, high, low):
    value_high, value_low = split(values)
    rows = values.shape[0]
    tall = dot(jnp.concatenate([value_high, value_low], axis=0), high)
    return tall[:rows] + tall[rows:] + dot(value_high, low)


def square_nt(values):
    high, low = split(values)
    return dot_nt(high, high) + (dot_nt(high, low) + dot_nt(low, high))


def iota(shape, dim):
    return lax.broadcasted_iota(jnp.int32, shape, dim)


def pad_rows(values, rows):
    missing = rows - values.shape[0]
    if missing == 0:
        return values
    return jnp.concatenate([values, jnp.zeros((missing, values.shape[1]), values.dtype)], axis=0)


def col_sum(values):
    return jnp.sum(values, axis=0, keepdims=True)


def kernel(
    groups, parts, capacity,
    deform_hbm, plastic_hbm, route_hbm, stiff_hbm, cubic_hbm, coupling_hbm, conn_ref,
    iface_hbm, load_hbm, average_hbm,
    stress_ref, field_ref,
    deform_ref, plastic_ref, route_ref, stiff_ref, cubic_ref, coupling_ref,
    iface_ref, load_ref, average_ref,
    whole, stiff_high, stiff_low,
    out_points, in_points, edge_out, edge_in,
    base_out, base_in, last_in, map_out, map_in, head_out, head_in,
    gram_buf, sum_buf, out_rows, in_rows,
    input_sem,
    point_send, point_recv, edge_send, edge_recv, ghost_send, ghost_recv,
    gram_send, gram_recv, sum_send, sum_recv, row_send, row_recv,
):
    group = lax.axis_index("macro")
    part = lax.axis_index("rve")
    blocks, slots, block = coupling_ref.shape[1], coupling_ref.shape[2], coupling_ref.shape[3]
    dofs = blocks * block
    comps, points = deform_ref.shape
    columns = groups * capacity

    barrier = pltpu.get_barrier_semaphore()
    for step in range(1, parts):
        pl.semaphore_signal(
            barrier, inc=1, device_id={"rve": lax.rem(part + step, parts)}, device_id_type=MESH
        )
    for step in range(1, groups):
        pl.semaphore_signal(
            barrier, inc=1, device_id={"macro": lax.rem(group + step, groups)}, device_id_type=MESH
        )

    loads = []
    for source, target in (
        (coupling_hbm, coupling_ref), (iface_hbm, iface_ref), (load_hbm, load_ref),
        (cubic_hbm, cubic_ref), (stiff_hbm, stiff_ref), (deform_hbm, deform_ref),
        (plastic_hbm, plastic_ref), (route_hbm, route_ref), (average_hbm, average_ref),
    ):
        loads.append(pltpu.make_async_copy(source, target, input_sem.at[len(loads)]))
        loads[-1].start()
    coupling_load, iface_load = loads[:2]
    early_loads, late_loads = loads[2:5], loads[5:]

    def exchange(source, target, send, recv):
        copies = []
        for step in range(1, groups):
            copies.append(pltpu.make_async_remote_copy(
                src_ref=source, dst_ref=target.at[group],
                send_sem=send.at[step - 1], recv_sem=recv.at[step - 1],
                device_id={"macro": lax.rem(group + step, groups)}, device_id_type=MESH,
            ))
            copies[-1].start()
        return copies

    def collect(buffer):
        owner = iota((16, columns), 1) // capacity
        found = jnp.zeros((16, columns), F32)
        for other in range(groups):
            shift = lax.rem(other + groups - group, groups) * capacity
            found = jnp.where(owner == other, pltpu.roll(buffer[other], shift, 1), found)
        return found

    def share(buffer, send, recv):
        copies = []
        for step in range(1, parts):
            copies.append(pltpu.make_async_remote_copy(
                src_ref=buffer.at[part], dst_ref=buffer.at[part],
                send_sem=send.at[step - 1], recv_sem=recv.at[step - 1],
                device_id={"rve": lax.rem(part + step, parts)}, device_id_type=MESH,
            ))
            copies[-1].start()
        return copies

    after, behind = lax.rem(part + 1, parts), lax.rem(part + parts - 1, parts)

    def push(source, target, peer, send, recv, place):
        copy = pltpu.make_async_remote_copy(
            src_ref=source, dst_ref=target, send_sem=send.at[place], recv_sem=recv.at[place],
            device_id={"rve": peer}, device_id_type=MESH,
        )
        copy.start()
        return copy

    def arrive(copies):
        for copy in copies:
            copy.wait_recv()

    def gathered(buffer):
        total = buffer[0]
        for other in range(1, parts):
            total = total + buffer[other]
        return total

    coupling_load.wait()
    lane = iota((block, LANES), 1) < block
    doubled = []
    for row in range(blocks):
        square = square_nt(coupling_ref[0, row].reshape(slots * block, block))
        doubled.append([])
        for slot in range(slots):
            spring = square[slot * block:(slot + 1) * block, slot * block:(slot + 1) * block]
            doubled[row].append(jnp.concatenate([spring, spring], axis=1))

    def mark(row, slot, far):
        if row == far:
            return jnp.float32(0.0)
        return jnp.where(conn_ref[0, slot, row] == far, 1.0, 0.0).astype(F32)

    for row in range(blocks):
        own = doubled[row][0]
        for slot in range(1, slots):
            own = own + doubled[row][slot]
        for other in range(blocks):
            if other != row:
                for slot in range(slots):
                    own = own + doubled[other][slot] * mark(other, slot, row)
        for pair in range(blocks // 2):
            left, right = 2 * pair, 2 * pair + 1
            value = jnp.zeros((block, LANES), F32)
            for slot in range(slots):
                value = value - doubled[row][slot] * jnp.where(
                    lane, mark(row, slot, left), mark(row, slot, right)
                )
                value = value - jnp.where(
                    lane, doubled[left][slot] * mark(left, slot, row),
                    doubled[right][slot] * mark(right, slot, row),
                )
            if row == left:
                value = value + jnp.where(lane, own, 0.0)
            if row == right:
                value = value + jnp.where(lane, 0.0, own)
            whole[row * block:(row + 1) * block, pair * LANES:(pair + 1) * LANES] = value

    iface_load.wait()
    for copy in early_loads:
        copy.wait()
    own_edge = iface_ref[0]
    own_spring = square_nt(own_edge)
    own_high, own_low = split(own_spring)
    diagonal = iota((dofs, dofs), 0) == iota((dofs, dofs), 1)
    stiffness = whole[...] + jnp.where(diagonal, stiff_ref[...], 0.0)
    high, low = split(stiffness)
    stiff_high[:dofs, :dofs] = high
    stiff_low[:dofs, :dofs] = low
    whole[dofs - block:, :] = stiffness[dofs - block:, :]
    high, low = split(stiffness[:block, :block] + own_spring)
    stiff_high[:block, :block] = high
    stiff_low[:block, :block] = low
    for target, spring in ((stiff_high, own_high), (stiff_low, own_low)):
        target[:dofs, dofs:] = jnp.zeros((dofs, 2 * block), BF16)
        target[dofs:, :] = jnp.zeros((16 + block, dofs + 2 * block), BF16)
        target[:block, dofs:dofs + block] = -spring
        target[dofs + 16:, :block] = spring

    maps = pad_rows(load_ref[:, 0, :], 16)
    cubic = pad_rows(cubic_ref[...], 16)

    def ends(values):
        return jnp.concatenate([values[:, :block], values[:, dofs - block:]], axis=1)

    image_map = apply_rows(maps, stiff_high[:dofs, :dofs], stiff_low[:dofs, :dofs])
    packed_rows = base_out.shape[0]
    packed = pad_rows(jnp.concatenate([maps[:comps], image_map[:comps], cubic[:1]], axis=0), packed_rows)
    base_out[...] = packed
    edge_out[:packed_rows, :] = ends(packed)
    edge_out[packed_rows:, :] = jnp.concatenate([own_edge[:block // 2], own_edge[block // 2:]], axis=1)

    pl.semaphore_wait(barrier, groups + parts - 2)

    sends = []
    edge_copies = [
        push(edge_out, edge_in.at[0], after, edge_send, edge_recv, 0),
        push(edge_out, edge_in.at[1], behind, edge_send, edge_recv, 1),
    ]

    ghost_copies = [
        push(base_out, base_in, after, ghost_send, ghost_recv, 0),
        push(whole.at[pl.ds(dofs - block, block)], last_in, after, ghost_send, ghost_recv, 1),
    ]

    for copy in late_loads:
        copy.wait()
    route = route_ref[...]
    hot = (iota((groups, points), 0) == route).astype(F32)
    before = (iota((points, points), 0) < iota((points, points), 1)).astype(BF16)
    rank = col_sum(hot * dot(hot.astype(BF16), before))
    slot_of = (route * capacity).astype(F32) + rank
    select = (iota((columns, points), 0).astype(F32) == slot_of).astype(F32)
    sent = pad_rows(
        jnp.concatenate([deform_ref[...], plastic_ref[...].astype(F32)], axis=0), 16
    )
    out_points[...] = dot_nt(sent, select, HIGHEST)
    point_copies = exchange(out_points, in_points, point_send, point_recv)
    sends += point_copies + edge_copies + ghost_copies
    in_points[group] = out_points[...]
    average_high, average_low = split(pad_rows(average_ref[:, 0, :], 16))
    stiff_high[dofs:dofs + 16, :dofs] = average_high
    stiff_low[dofs:dofs + 16, :dofs] = average_low

    arrive(edge_copies)
    packed = edge_in[1, packed_rows:, :]
    next_spring = square_nt(jnp.concatenate([packed[:, :block], packed[:, block:]], axis=0))
    next_high, next_low = split(next_spring)
    high, low = split(stiffness[dofs - block:, dofs - block:] + next_spring)
    stiff_high[dofs - block:dofs, dofs - block:dofs] = high
    stiff_low[dofs - block:dofs, dofs - block:dofs] = low
    stiff_high[dofs - block:dofs, dofs + block:] = -next_high
    stiff_low[dofs - block:dofs, dofs + block:] = -next_low

    def own_rows(values):
        return apply_rows(values, own_high, own_low)

    def next_rows(values):
        return apply_rows(values, next_high, next_low)

    def unpack(values):
        return jnp.concatenate([
            pad_rows(values[:comps], 16), pad_rows(values[comps:2 * comps], 16),
            pad_rows(values[2 * comps:2 * comps + 1], 16),
        ], axis=0)

    prev_edge, next_edge = unpack(edge_in[0, :packed_rows]), unpack(edge_in[1, :packed_rows])
    prev_map, next_map = prev_edge[0:16, block:], next_edge[0:16, :block]
    first_map, last_map = maps[:, :block], maps[:, dofs - block:]
    through_own = own_rows(jnp.concatenate([prev_map, first_map], axis=0))
    through_next = next_rows(jnp.concatenate([next_map, last_map], axis=0))
    prev_image = prev_edge[16:32, block:] + through_own[:16] - through_own[16:]
    next_image = next_edge[16:32, :block] - through_next[16:]
    image_map = jnp.concatenate([
        image_map[:, :block] - through_own[:16],
        image_map[:, block:dofs - block],
        image_map[:, dofs - block:] + through_next[16:] - through_next[:16],
    ], axis=1)
    second_map = apply_rows(image_map, stiff_high[:dofs, :dofs], stiff_low[:dofs, :dofs])
    second_map = jnp.concatenate([
        second_map[:, :block] - own_rows(prev_image),
        second_map[:, block:dofs - block],
        second_map[:, dofs - block:] - next_rows(next_image),
    ], axis=1)
    basis = jnp.concatenate([maps, image_map, second_map], axis=0)
    products = dot_nt(basis[0:32], basis, HIGHEST)
    gram_buf[part] = jnp.concatenate([
        products[0:16, 0:32], products[16:32, 16:48], image_map[:, :block],
    ], axis=1)
    map_out[...] = second_map
    head_out[...] = second_map[:, :LANES]
    map_copies = [
        push(map_out, map_in, after, ghost_send, ghost_recv, 2),
        push(head_out, head_in, behind, ghost_send, ghost_recv, 3),
    ]
    gram_copies = share(gram_buf, gram_send, gram_recv)
    sends += map_copies + gram_copies

    def early_cols(map_rows, image_rows, cubic_rows):
        map_high, map_low = split(map_rows)
        image_high, image_low = split(image_rows)
        both_high = jnp.concatenate([map_high, image_high], axis=0).astype(F32)
        both_low = jnp.concatenate([map_low, image_low], axis=0).astype(F32)
        rows = jnp.concatenate([both_high, both_high, both_low, pad_rows(cubic_rows, 32)], axis=0)
        cols = jnp.transpose(rows)
        return cols.astype(BF16), cols[:, 96:97]

    def late_cols(second_rows, image_rows):
        second_high, second_low = split(second_rows)
        image_high, image_low = split(image_rows)
        return jnp.transpose(jnp.concatenate([
            second_high, second_high, second_low, image_high, image_high, image_low,
            jnp.zeros((32, second_rows.shape[1]), BF16),
        ], axis=0))

    own_early, own_cubic = early_cols(maps, image_map, cubic)
    own_late = late_cols(second_map, jnp.zeros_like(second_map))
    arrive(point_copies)
    received = collect(in_points)
    flag = received[comps:comps + 1]
    strain = jnp.where(iota((16, columns), 0) < comps, received, 0.0)
    hard = own_cubic * flag

    arrive(ghost_copies)
    prev_rows = unpack(base_in[...])
    last_rows = last_in[...]
    last_high, last_low = split(jnp.concatenate([
        last_rows[:, :dofs - LANES],
        last_rows[:, dofs - LANES:] + jnp.concatenate([jnp.zeros_like(own_spring), own_spring], axis=1),
    ], axis=1))
    ghost_early, ghost_cubic = early_cols(
        jnp.concatenate([prev_rows[0:16], next_map], axis=1),
        jnp.concatenate([
            jnp.zeros((16, block), F32), prev_rows[16:32, block:dofs - block], prev_image, next_image,
        ], axis=1),
        jnp.concatenate([prev_rows[32:48], next_edge[32:48, :block]], axis=1),
    )
    ghost_hard = ghost_cubic * flag

    arrive(gram_copies + map_copies)
    ghost_late = late_cols(
        jnp.concatenate([map_in[...], head_in[...][:, :block]], axis=1),
        jnp.concatenate([gram_buf[behind][:, block:], jnp.zeros((16, dofs), F32)], axis=1),
    )
    gram = gathered(gram_buf)
    forms = jnp.concatenate(
        [gram[0:16, 0:16], gram[0:16, 16:32], gram[0:16, 32:48], gram[0:16, 48:64]], axis=0
    )
    forms = jnp.dot(forms, strain, precision=HIGHEST, preferred_element_type=F32)
    norm = col_sum(forms[0:16] * strain)
    curve = col_sum(forms[16:32] * strain)
    third = col_sum(forms[32:48] * strain)
    fourth = col_sum(forms[48:64] * strain)

    def second_step(norm, curve, left_norm, left_curve, cross):
        ratio = left_norm / (norm + EPSILON)
        next_curve = left_curve + ratio * (2.0 * cross + ratio * curve)
        next_curve = jnp.maximum(next_curve, 0.09 * left_norm)
        next_len = left_norm / (next_curve + EPSILON)
        return next_len, next_len * ratio

    step_len = norm / (curve + EPSILON)
    left_norm = jnp.maximum(norm - step_len * (2.0 * curve - step_len * third), 0.0)
    left_curve = curve - step_len * (2.0 * third - step_len * fourth)
    cross = curve - step_len * third
    next_len, carried = second_step(norm, curve, left_norm, left_curve, cross)
    along = step_len + carried + next_len
    across = next_len * step_len
    weights = jnp.concatenate([
        jnp.concatenate([along * strain, -across * strain, jnp.zeros_like(strain)], axis=0),
        jnp.concatenate([strain, -along * strain, across * strain], axis=0),
    ], axis=1)
    weight_high, weight_low = split(weights)
    blank = jnp.zeros((32, 2 * columns), BF16)
    both = dot(
        jnp.concatenate([
            jnp.concatenate([own_early, own_late], axis=1), jnp.concatenate([ghost_early, ghost_late], axis=1),
        ], axis=0),
        jnp.concatenate([
            weight_high[:32], weight_low[:32], weight_high[:32], blank,
            weight_high[32:], weight_low[32:], weight_high[32:],
            weight_high[16:32], weight_low[16:32], weight_high[16:32], blank,
        ], axis=0),
    )
    solved = both[:dofs, :columns]
    hard_square = hard * solved * solved
    tangent = 3.0 * hard_square
    residue = both[:dofs, columns:] - hard_square * solved
    ghost_solved = both[dofs:, :columns]
    ghost_square = ghost_hard * ghost_solved * ghost_solved
    ghost = both[dofs:, columns:] - ghost_square * ghost_solved
    own_product = apply_split(
        stiff_high[...], stiff_low[...], jnp.concatenate([residue, ghost[dofs - block:]], axis=0)
    )
    last_product = apply_split(last_high, last_low, ghost[:dofs])
    image = own_product[:dofs] + tangent * residue
    last_residue = ghost[dofs - block:dofs]
    last_image = (
        last_product + 3.0 * ghost_square[dofs - block:dofs] * last_residue - own_product[dofs + 16:]
    )
    image_product = apply_split(
        stiff_high[...], stiff_low[...],
        jnp.concatenate([image, 2.0 * last_image, jnp.zeros_like(last_image)], axis=0),
    )

    scaled = SCALE * image
    length = jnp.sqrt(col_sum(scaled * scaled))
    inverse = jnp.where(length > 0.0, SCALE / jnp.where(length > 0.0, length, 1.0), 0.0)
    length = length * (1.0 / SCALE)
    unit = inverse * image
    along_unit = col_sum(residue * unit)
    rest = residue - along_unit * unit
    form_unit = inverse * (image_product[:dofs] + tangent * image)
    form_rest = jnp.concatenate([
        image[:block] - apply_split(own_high, own_low, last_residue), image[block:dofs - block],
        image[dofs - block:] + apply_split(next_high, next_low, ghost[dofs:]),
    ], axis=0) - along_unit * form_unit
    sum_buf[part] = pad_rows(jnp.concatenate([
        col_sum(residue * residue), length, along_unit, col_sum(rest * rest),
        col_sum(rest * form_rest), col_sum(rest * form_unit + unit * form_rest), col_sum(unit * form_unit),
        jnp.zeros((1, columns), F32),
        apply_split(average_high, average_low, solved)[:comps],
        own_product[dofs:dofs + comps], image_product[dofs:dofs + comps],
    ], axis=0), sum_buf.shape[1])
    sum_copies = share(sum_buf, sum_send, sum_recv)
    sends += sum_copies
    arrive(sum_copies)
    sums = [sum_buf[other] for other in range(parts)]
    means = sum(sums[1:], sums[0])[8:]
    norm = sum(each[0:1] for each in sums)
    curve = sum(each[1:2] * each[2:3] for each in sums)
    step_len = norm / (curve + EPSILON)
    left_norm, left_curve, cross = 0.0, 0.0, 0.0
    for each in sums:
        beyond = step_len * each[1:2] - each[2:3]
        left_norm = left_norm + (each[3:4] + beyond * beyond)
        left_curve = left_curve + (each[4:5] - beyond * (each[5:6] - beyond * each[6:7]))
        cross = cross - beyond * each[1:2]
    next_len, carried = second_step(norm, curve, left_norm, left_curve, cross)
    along = step_len + carried
    total = (
        means[:comps] + along * means[comps:2 * comps]
        + next_len * (means[comps:2 * comps] - step_len * means[2 * comps:3 * comps])
    )

    out_rows[...] = pad_rows(total, 16)
    row_copies = exchange(out_rows, in_rows, row_send, row_recv)
    sends += row_copies
    in_rows[group] = out_rows[...]
    field_ref[0] = solved + along * residue + next_len * (residue - step_len * image)
    arrive(row_copies)
    back = collect(in_rows)
    back_high, back_low = split(back)
    back_rest = (back - back_high.astype(F32) - back_low.astype(F32)).astype(BF16)
    picked = dot(jnp.concatenate([back_high, back_low, back_rest], axis=0), select.astype(BF16))
    stress_ref[...] = (picked[:16] + (picked[16:32] + picked[32:]))[:comps]
    for copy in sends:
        copy.wait_send()


def place(stress_ref, field_ref, stress_out, field_out, sem):
    first = pltpu.make_async_copy(field_ref, field_out, sem.at[0])
    second = pltpu.make_async_copy(stress_ref, stress_out, sem.at[1])
    first.start()
    second.start()
    first.wait()
    second.wait()


def solution(mesh):
    groups, parts = mesh.shape["macro"], mesh.shape["rve"]

    def shards(deform, plastic, route, stiff, cubic, coupling, conn, iface, load_map, average_map):
        comps, points = deform.shape
        blocks, block = coupling.shape[1], coupling.shape[3]
        dofs = blocks * block
        capacity = 2 * points // groups
        columns = groups * capacity
        edge_rows = -(-(2 * comps + 1) // 8) * 8
        vmem = pl.BlockSpec(memory_space=pltpu.VMEM)
        hbm = pl.BlockSpec(memory_space=pltpu.HBM)
        dma = pltpu.SemaphoreType.DMA
        stress, field = pl.pallas_call(
            functools.partial(kernel, groups, parts, capacity),
            out_shape=(
                pltpu.VMEM((comps, points), F32),
                pltpu.VMEM((1, dofs, columns), F32),
            ),
            in_specs=[hbm] * 6 + [pl.BlockSpec(memory_space=pltpu.SMEM)] + [hbm] * 3,
            out_specs=(vmem, vmem),
            scratch_shapes=[
                pltpu.VMEM(deform.shape, F32),
                pltpu.VMEM((1, points), jnp.int32),
                pltpu.VMEM((1, points), jnp.int32),
                pltpu.VMEM((1, dofs), F32),
                pltpu.VMEM((1, dofs), F32),
                pltpu.VMEM(coupling.shape, F32),
                pltpu.VMEM(iface.shape, F32),
                pltpu.VMEM((comps, 1, dofs), F32),
                pltpu.VMEM((comps, 1, dofs), F32),
                pltpu.VMEM((dofs, dofs), F32),
                pltpu.VMEM((dofs + 16 + block, dofs + 2 * block), BF16),
                pltpu.VMEM((dofs + 16 + block, dofs + 2 * block), BF16),
                pltpu.VMEM((16, columns), F32),
                pltpu.VMEM((groups, 16, columns), F32),
                pltpu.VMEM((edge_rows + block // 2, LANES), F32),
                pltpu.VMEM((2, edge_rows + block // 2, LANES), F32),
                pltpu.VMEM((edge_rows, dofs), F32),
                pltpu.VMEM((edge_rows, dofs), F32),
                pltpu.VMEM((block, dofs), F32),
                pltpu.VMEM((16, dofs), F32),
                pltpu.VMEM((16, dofs), F32),
                pltpu.VMEM((16, LANES), F32),
                pltpu.VMEM((16, LANES), F32),
                pltpu.VMEM((parts, 16, LANES), F32),
                pltpu.VMEM((parts, -(-(8 + 3 * comps) // 8) * 8, columns), F32),
                pltpu.VMEM((16, columns), F32),
                pltpu.VMEM((groups, 16, columns), F32),
                dma((9,)),
                dma((groups - 1,)), dma((groups - 1,)),
                dma((2,)), dma((2,)),
                dma((4,)), dma((4,)),
                dma((parts - 1,)), dma((parts - 1,)),
                dma((parts - 1,)), dma((parts - 1,)),
                dma((groups - 1,)), dma((groups - 1,)),
            ],
            compiler_params=pltpu.CompilerParams(
                collective_id=0, has_side_effects=True, vmem_limit_bytes=60 * 1024 * 1024
            ),
        )(
            deform, plastic[None], route[None], stiff, cubic, coupling,
            jnp.transpose(conn, (0, 2, 1)), iface,
            jnp.transpose(load_map, (1, 0, 2)), jnp.transpose(average_map, (1, 0, 2)),
        )
        return pl.pallas_call(
            place,
            out_shape=(
                jax.ShapeDtypeStruct((comps, points), F32),
                jax.ShapeDtypeStruct((1, dofs, columns), F32),
            ),
            in_specs=[vmem, vmem], out_specs=(hbm, hbm),
            scratch_shapes=[dma((2,))],
        )(*(pltpu.with_memory_space_constraint(x, pltpu.VMEM) for x in (stress, field)))

    return jax.shard_map(
        shards,
        mesh=mesh,
        in_specs=(
            P(None, "macro"),
            P("macro"),
            P("macro"),
            P("macro", "rve"),
            P("macro", "rve"),
            P("macro", "rve", None, None, None),
            P("macro", "rve", None),
            P("macro", "rve", None),
            P("macro", None, "rve"),
            P("macro", None, "rve"),
        ),
        out_specs=(P(None, "macro"), P("macro", "rve", None)),
        check_vma=False,
    )
```

```python
import functools

import jax
import jax.numpy as jnp
from jax import lax
from jax.experimental import pallas as pl
from jax.experimental.pallas import tpu as pltpu
from jax.sharding import PartitionSpec as P

EPSILON = 1e-06
SCALE = 2.0 ** -20
MESH = pl.DeviceIdType.MESH
HIGHEST = lax.Precision.HIGHEST
F32 = jnp.float32
BF16 = jnp.bfloat16
LANES = 128
NT = (((1,), (1,)), ((), ()))


def split(values):
    high = values.astype(BF16)
    return high, (values - high.astype(F32)).astype(BF16)


def dot(left, right):
    return jnp.dot(left, right, preferred_element_type=F32)


def dot_nt(left, right, precision=None):
    return lax.dot_general(left, right, NT, precision=precision, preferred_element_type=F32)


def apply_split(high, low, values):
    value_high, value_low = split(values)
    width = values.shape[1]
    wide = dot(high, jnp.concatenate([value_high, value_low], axis=1))
    return wide[:, :width] + wide[:, width:] + dot(low, value_high)


def apply_rows(values, high, low):
    value_high, value_low = split(values)
    rows = values.shape[0]
    tall = dot(jnp.concatenate([value_high, value_low], axis=0), high)
    return tall[:rows] + tall[rows:] + dot(value_high, low)


def dot_nt_split(left, right):
    left_high, left_low = split(left)
    right_high, right_low = split(right)
    rows = left.shape[0]
    tall = dot_nt(jnp.concatenate([left_high, left_low], axis=0), right_high)
    return tall[:rows] + tall[rows:] + dot_nt(left_high, right_low)


def square_nt(values):
    high, low = split(values)
    return dot_nt(high, high) + (dot_nt(high, low) + dot_nt(low, high))


def iota(shape, dim):
    return lax.broadcasted_iota(jnp.int32, shape, dim)


def pad_rows(values, rows):
    missing = rows - values.shape[0]
    if missing == 0:
        return values
    return jnp.concatenate([values, jnp.zeros((missing, values.shape[1]), values.dtype)], axis=0)


def col_sum(values):
    return jnp.sum(values, axis=0, keepdims=True)


def kernel(
    groups, parts, capacity,
    deform_hbm, plastic_hbm, route_hbm, stiff_hbm, cubic_hbm, coupling_hbm, conn_ref,
    iface_hbm, load_hbm, average_hbm,
    stress_ref, field_ref,
    deform_ref, plastic_ref, route_ref, stiff_ref, cubic_ref, coupling_ref,
    iface_ref, load_ref, average_ref,
    whole, stiff_high, stiff_low,
    out_points, in_points, edge_out, prev_in, next_in,
    base_out, base_in, last_in, map_out, map_in, head_out, head_in,
    gram_buf, sum_buf, out_rows, in_rows,
    input_sem,
    point_send, point_recv, edge_send, edge_recv, ghost_send, ghost_recv,
    gram_send, gram_recv, sum_send, sum_recv, row_send, row_recv,
):
    group = lax.axis_index("macro")
    part = lax.axis_index("rve")
    blocks, slots, block = coupling_ref.shape[1], coupling_ref.shape[2], coupling_ref.shape[3]
    dofs = blocks * block
    comps, points = deform_ref.shape
    columns = groups * capacity

    barrier = pltpu.get_barrier_semaphore()
    for step in range(1, parts):
        pl.semaphore_signal(
            barrier, inc=1, device_id={"rve": lax.rem(part + step, parts)}, device_id_type=MESH
        )
    for step in range(1, groups):
        pl.semaphore_signal(
            barrier, inc=1, device_id={"macro": lax.rem(group + step, groups)}, device_id_type=MESH
        )

    loads = []
    for source, target in (
        (coupling_hbm, coupling_ref), (iface_hbm, iface_ref), (load_hbm, load_ref),
        (cubic_hbm, cubic_ref), (stiff_hbm, stiff_ref), (deform_hbm, deform_ref),
        (plastic_hbm, plastic_ref), (route_hbm, route_ref), (average_hbm, average_ref),
    ):
        loads.append(pltpu.make_async_copy(source, target, input_sem.at[len(loads)]))
        loads[-1].start()
    coupling_load, iface_load = loads[:2]
    early_loads, late_loads = loads[2:5], loads[5:]

    def exchange(source, target, send, recv):
        copies = []
        for step in range(1, groups):
            copies.append(pltpu.make_async_remote_copy(
                src_ref=source, dst_ref=target.at[group],
                send_sem=send.at[step - 1], recv_sem=recv.at[step - 1],
                device_id={"macro": lax.rem(group + step, groups)}, device_id_type=MESH,
            ))
            copies[-1].start()
        return copies

    def collect(buffer):
        owner = iota((16, columns), 1) // capacity
        found = jnp.zeros((16, columns), F32)
        for other in range(groups):
            shift = lax.rem(other + groups - group, groups) * capacity
            found = jnp.where(owner == other, pltpu.roll(buffer[other], shift, 1), found)
        return found

    def share(buffer, send, recv):
        copies = []
        for step in range(1, parts):
            copies.append(pltpu.make_async_remote_copy(
                src_ref=buffer.at[part], dst_ref=buffer.at[part],
                send_sem=send.at[step - 1], recv_sem=recv.at[step - 1],
                device_id={"rve": lax.rem(part + step, parts)}, device_id_type=MESH,
            ))
            copies[-1].start()
        return copies

    after, behind = lax.rem(part + 1, parts), lax.rem(part + parts - 1, parts)

    def push(source, target, peer, send, recv, place):
        copy = pltpu.make_async_remote_copy(
            src_ref=source, dst_ref=target, send_sem=send.at[place], recv_sem=recv.at[place],
            device_id={"rve": peer}, device_id_type=MESH,
        )
        copy.start()
        return copy

    def arrive(copies):
        for copy in copies:
            copy.wait_recv()

    def gathered(buffer):
        total = buffer[0]
        for other in range(1, parts):
            total = total + buffer[other]
        return total

    coupling_load.wait()
    lane = iota((block, LANES), 1) < block
    doubled = []
    for row in range(blocks):
        square = square_nt(coupling_ref[0, row].reshape(slots * block, block))
        doubled.append([])
        for slot in range(slots):
            spring = square[slot * block:(slot + 1) * block, slot * block:(slot + 1) * block]
            doubled[row].append(jnp.concatenate([spring, spring], axis=1))

    def mark(row, slot, far):
        if row == far:
            return jnp.float32(0.0)
        return jnp.where(conn_ref[0, slot, row] == far, 1.0, 0.0).astype(F32)

    for row in range(blocks):
        own = doubled[row][0]
        for slot in range(1, slots):
            own = own + doubled[row][slot]
        for other in range(blocks):
            if other != row:
                for slot in range(slots):
                    own = own + doubled[other][slot] * mark(other, slot, row)
        for pair in range(blocks // 2):
            left, right = 2 * pair, 2 * pair + 1
            value = jnp.zeros((block, LANES), F32)
            for slot in range(slots):
                value = value - doubled[row][slot] * jnp.where(
                    lane, mark(row, slot, left), mark(row, slot, right)
                )
                value = value - jnp.where(
                    lane, doubled[left][slot] * mark(left, slot, row),
                    doubled[right][slot] * mark(right, slot, row),
                )
            if row == left:
                value = value + jnp.where(lane, own, 0.0)
            if row == right:
                value = value + jnp.where(lane, 0.0, own)
            whole[row * block:(row + 1) * block, pair * LANES:(pair + 1) * LANES] = value

    iface_load.wait()
    for copy in early_loads:
        copy.wait()
    own_edge = iface_ref[0]
    own_spring = square_nt(own_edge)
    own_high, own_low = split(own_spring)
    diagonal = iota((dofs, dofs), 0) == iota((dofs, dofs), 1)
    stiffness = whole[...] + jnp.where(diagonal, stiff_ref[...], 0.0)
    high, low = split(stiffness)
    stiff_high[:dofs, :dofs] = high
    stiff_low[:dofs, :dofs] = low
    whole[dofs - block:, :] = stiffness[dofs - block:, :]
    high, low = split(stiffness[:block, :block] + own_spring)
    stiff_high[:block, :block] = high
    stiff_low[:block, :block] = low
    for target, spring in ((stiff_high, own_high), (stiff_low, own_low)):
        target[:dofs, dofs:] = jnp.zeros((dofs, 2 * block), BF16)
        target[dofs:, :] = jnp.zeros((16 + block, dofs + 2 * block), BF16)
        target[:block, dofs:dofs + block] = -spring
        target[dofs + 16:, :block] = spring

    maps = pad_rows(load_ref[:, 0, :], 16)
    cubic = pad_rows(cubic_ref[...], 16)

    def ends(values):
        return jnp.concatenate([values[:, :block], values[:, dofs - block:]], axis=1)

    image_map = apply_rows(maps, stiff_high[:dofs, :dofs], stiff_low[:dofs, :dofs])
    base_out[...] = pad_rows(
        jnp.concatenate([maps[:comps], image_map[:comps], cubic[:1]], axis=0), base_out.shape[0]
    )
    edge_out[:40, :] = ends(jnp.concatenate([maps, image_map, cubic[:8]], axis=0))
    edge_out[40:, :] = jnp.concatenate([own_edge[:block // 2], own_edge[block // 2:]], axis=1)

    pl.semaphore_wait(barrier, groups + parts - 2)

    sends = []
    edge_copies = [
        push(edge_out.at[pl.ds(0, 40)], prev_in, after, edge_send, edge_recv, 0),
        push(edge_out, next_in, behind, edge_send, edge_recv, 1),
    ]

    ghost_copies = [
        push(base_out, base_in, after, ghost_send, ghost_recv, 0),
        push(whole.at[pl.ds(dofs - block, block)], last_in, after, ghost_send, ghost_recv, 1),
    ]

    for copy in late_loads:
        copy.wait()
    route = route_ref[...]
    hot = (iota((groups, points), 0) == route).astype(F32)
    before = (iota((points, points), 0) < iota((points, points), 1)).astype(BF16)
    rank = col_sum(hot * dot(hot.astype(BF16), before))
    slot_of = (route * capacity).astype(F32) + rank
    select = (iota((columns, points), 0).astype(F32) == slot_of).astype(F32)
    sent = pad_rows(
        jnp.concatenate([deform_ref[...], plastic_ref[...].astype(F32)], axis=0), 16
    )
    out_points[...] = dot_nt(sent, select, HIGHEST)
    point_copies = exchange(out_points, in_points, point_send, point_recv)
    sends += point_copies + edge_copies + ghost_copies
    in_points[group] = out_points[...]
    averages = pad_rows(average_ref[:, 0, :], 16)
    average_high, average_low = split(averages)
    stiff_high[dofs:dofs + 16, :dofs] = average_high
    stiff_low[dofs:dofs + 16, :dofs] = average_low

    def own_rows(values):
        return apply_rows(values, own_high, own_low)

    def next_rows(values):
        return apply_rows(values, next_high, next_low)

    def unpack(values):
        return jnp.concatenate([
            pad_rows(values[:comps], 16), pad_rows(values[comps:2 * comps], 16),
            pad_rows(values[2 * comps:2 * comps + 1], 16),
        ], axis=0)

    first_map, last_map = maps[:, :block], maps[:, dofs - block:]
    through_first = own_rows(first_map)
    second_map = apply_rows(image_map, stiff_high[:dofs, :dofs], stiff_low[:dofs, :dofs])
    ends_high = jnp.concatenate([stiff_high[:block, :dofs], stiff_high[dofs - block:dofs, :dofs]], axis=0)
    ends_low = jnp.concatenate([stiff_low[:block, :dofs], stiff_low[dofs - block:dofs, :dofs]], axis=0)

    arrive(edge_copies)
    packed = next_in[40:, :]
    next_spring = square_nt(jnp.concatenate([packed[:, :block], packed[:, block:]], axis=0))
    next_high, next_low = split(next_spring)
    prev_map, next_map = prev_in[0:16, block:], next_in[0:16, :block]
    through_prev = own_rows(prev_map)
    through_next = next_rows(jnp.concatenate([last_map - next_map, last_map], axis=0))
    prev_image = prev_in[16:32, block:] + through_prev - through_first
    next_image = next_in[16:32, :block] - through_next[16:]
    change = jnp.concatenate([-through_prev, through_next[:16]], axis=1)
    image_map = jnp.concatenate([
        image_map[:, :block] + change[:, :block],
        image_map[:, block:dofs - block],
        image_map[:, dofs - block:] + change[:, block:],
    ], axis=1)
    second_map = second_map + apply_rows(change, ends_high, ends_low)
    second_map = jnp.concatenate([
        second_map[:, :block] - own_rows(prev_image),
        second_map[:, block:dofs - block],
        second_map[:, dofs - block:] + next_rows(image_map[:, dofs - block:] - next_image),
    ], axis=1)
    products = dot_nt_split(
        jnp.concatenate([maps, image_map, averages], axis=0),
        jnp.concatenate([maps, image_map, second_map], axis=0),
    )
    gram_buf[part] = jnp.concatenate([
        products[0:16, 0:32], products[16:32, 16:48], products[32:48], jnp.zeros((16, 16), F32),
    ], axis=1)
    map_out[:, :dofs] = second_map
    map_out[:, dofs:] = jnp.concatenate([image_map[:, :block], jnp.zeros((16, block), F32)], axis=1)
    head_out[...] = second_map[:, :LANES]
    gram_copies = share(gram_buf, gram_send, gram_recv)
    map_copies = [
        push(map_out, map_in, after, ghost_send, ghost_recv, 2),
        push(head_out, head_in, behind, ghost_send, ghost_recv, 3),
    ]
    sends += map_copies + gram_copies
    high, low = split(stiffness[dofs - block:, dofs - block:] + next_spring)
    stiff_high[dofs - block:dofs, dofs - block:dofs] = high
    stiff_low[dofs - block:dofs, dofs - block:dofs] = low
    stiff_high[dofs - block:dofs, dofs + block:] = -next_high
    stiff_low[dofs - block:dofs, dofs + block:] = -next_low

    def early_cols(map_rows, image_rows, cubic_rows):
        map_high, map_low = split(map_rows)
        image_high, image_low = split(image_rows)
        both_high = jnp.concatenate([map_high, image_high], axis=0).astype(F32)
        both_low = jnp.concatenate([map_low, image_low], axis=0).astype(F32)
        rows = jnp.concatenate([both_high, both_high, both_low, pad_rows(cubic_rows, 32)], axis=0)
        cols = jnp.transpose(rows)
        return cols.astype(BF16), cols[:, 96:97]

    def late_cols(second_rows, image_rows):
        second_high, second_low = split(second_rows)
        image_high, image_low = split(image_rows)
        return jnp.transpose(jnp.concatenate([
            second_high, second_high, second_low, image_high, image_high, image_low,
            jnp.zeros((32, second_rows.shape[1]), BF16),
        ], axis=0))

    own_early, own_cubic = early_cols(maps, image_map, cubic)
    own_late = late_cols(second_map, jnp.zeros_like(second_map))
    arrive(point_copies)
    received = collect(in_points)
    flag = received[comps:comps + 1]
    strain = jnp.where(iota((16, columns), 0) < comps, received, 0.0)
    strain_high, strain_low = split(strain)
    hard = own_cubic * flag

    arrive(ghost_copies)
    prev_rows = unpack(base_in[...])
    last_rows = last_in[...]
    last_high, last_low = split(jnp.concatenate([
        last_rows[:, :dofs - LANES],
        last_rows[:, dofs - LANES:] + jnp.concatenate([jnp.zeros_like(own_spring), own_spring], axis=1),
    ], axis=1))
    ghost_early, ghost_cubic = early_cols(
        jnp.concatenate([prev_rows[0:16], next_map], axis=1),
        jnp.concatenate([
            jnp.zeros((16, block), F32), prev_rows[16:32, block:dofs - block], prev_image, next_image,
        ], axis=1),
        jnp.concatenate([prev_rows[32:40], next_in[32:40, :block]], axis=1),
    )
    ghost_hard = ghost_cubic * flag

    arrive(gram_copies)
    gram = gathered(gram_buf)
    form_high, form_low = split(jnp.concatenate(
        [gram[:, 0:16], gram[:, 16:32], gram[:, 32:48], gram[:, 48:64]], axis=0
    ))
    wide = dot(
        jnp.concatenate([form_high, form_low], axis=0), jnp.concatenate([strain_high, strain_low], axis=1)
    )
    forms = wide[:64, :columns] + (wide[:64, columns:] + wide[64:, :columns])
    norm = col_sum(forms[0:16] * strain)
    curve = col_sum(forms[16:32] * strain)
    third = col_sum(forms[32:48] * strain)
    fourth = col_sum(forms[48:64] * strain)

    def second_step(norm, curve, left_norm, left_curve, cross):
        ratio = left_norm / (norm + EPSILON)
        next_curve = left_curve + ratio * (2.0 * cross + ratio * curve)
        next_curve = jnp.maximum(next_curve, 0.09 * left_norm)
        next_len = left_norm / (next_curve + EPSILON)
        return next_len, next_len * ratio

    step_len = norm / (curve + EPSILON)
    left_norm = jnp.maximum(norm - step_len * (2.0 * curve - step_len * third), 0.0)
    left_curve = curve - step_len * (2.0 * third - step_len * fourth)
    cross = curve - step_len * third
    next_len, carried = second_step(norm, curve, left_norm, left_curve, cross)
    along = step_len + carried + next_len
    across = next_len * step_len
    weights = jnp.concatenate([
        jnp.concatenate([along * strain, -across * strain, jnp.zeros_like(strain)], axis=0),
        jnp.concatenate([strain, -along * strain, across * strain], axis=0),
    ], axis=1)
    weight_high, weight_low = split(weights)
    arrive(map_copies)
    ghost_late = late_cols(
        jnp.concatenate([map_in[:, :dofs], head_in[:, :block]], axis=1),
        jnp.concatenate([map_in[:, dofs:dofs + block], jnp.zeros((16, dofs), F32)], axis=1),
    )
    blank = jnp.zeros((32, 2 * columns), BF16)
    both = dot(
        jnp.concatenate([
            jnp.concatenate([own_early, own_late], axis=1), jnp.concatenate([ghost_early, ghost_late], axis=1),
        ], axis=0),
        jnp.concatenate([
            weight_high[:32], weight_low[:32], weight_high[:32], blank,
            weight_high[32:], weight_low[32:], weight_high[32:],
            weight_high[16:32], weight_low[16:32], weight_high[16:32], blank,
        ], axis=0),
    )
    solved = both[:dofs, :columns]
    hard_square = hard * solved * solved
    tangent = 3.0 * hard_square
    residue = both[:dofs, columns:] - hard_square * solved
    ghost_solved = both[dofs:, :columns]
    ghost_square = ghost_hard * ghost_solved * ghost_solved
    ghost = both[dofs:, columns:] - ghost_square * ghost_solved
    own_product = apply_split(
        stiff_high[...], stiff_low[...], jnp.concatenate([residue, ghost[dofs - block:]], axis=0)
    )
    last_product = apply_split(last_high, last_low, ghost[:dofs])
    image = own_product[:dofs] + tangent * residue
    last_residue = ghost[dofs - block:dofs]
    last_image = (
        last_product + 3.0 * ghost_square[dofs - block:dofs] * last_residue - own_product[dofs + 16:]
    )
    image_product = apply_split(
        stiff_high[...], stiff_low[...],
        jnp.concatenate([image, 2.0 * last_image, jnp.zeros_like(last_image)], axis=0),
    )

    scaled = SCALE * image
    length = jnp.sqrt(col_sum(scaled * scaled))
    inverse = jnp.where(length > 0.0, SCALE / jnp.where(length > 0.0, length, 1.0), 0.0)
    length = length * (1.0 / SCALE)
    unit = inverse * image
    along_unit = col_sum(residue * unit)
    rest = residue - along_unit * unit
    form_unit = inverse * (image_product[:dofs] + tangent * image)
    form_rest = jnp.concatenate([
        image[:block] - apply_split(own_high, own_low, last_residue), image[block:dofs - block],
        image[dofs - block:] + apply_split(next_high, next_low, ghost[dofs:]),
    ], axis=0) - along_unit * form_unit
    sum_buf[part] = pad_rows(jnp.concatenate([
        length, along_unit, col_sum(rest * rest),
        col_sum(rest * form_rest), col_sum(rest * form_unit + unit * form_rest), col_sum(unit * form_unit),
        own_product[dofs:dofs + comps], image_product[dofs:dofs + comps],
    ], axis=0), sum_buf.shape[1])
    sum_copies = share(sum_buf, sum_send, sum_recv)
    sends += sum_copies
    solved_means = jnp.dot(
        gram[:, 64:112], weights[:, :columns], precision=HIGHEST, preferred_element_type=F32
    )[:comps]
    arrive(sum_copies)
    sums = [sum_buf[other] for other in range(parts)]
    means = sum(sums[1:], sums[0])[6:]
    norm = sum(each[2:3] + each[1:2] * each[1:2] for each in sums)
    curve = sum(each[0:1] * each[1:2] for each in sums)
    step_len = norm / (curve + EPSILON)
    left_norm, left_curve, cross = 0.0, 0.0, 0.0
    for each in sums:
        beyond = step_len * each[0:1] - each[1:2]
        left_norm = left_norm + (each[2:3] + beyond * beyond)
        left_curve = left_curve + (each[3:4] - beyond * (each[4:5] - beyond * each[5:6]))
        cross = cross - beyond * each[0:1]
    next_len, carried = second_step(norm, curve, left_norm, left_curve, cross)
    along = step_len + carried
    total = (
        solved_means + along * means[:comps]
        + next_len * (means[:comps] - step_len * means[comps:2 * comps])
    )

    out_rows[...] = pad_rows(total, 16)
    row_copies = exchange(out_rows, in_rows, row_send, row_recv)
    in_rows[group] = out_rows[...]
    field_ref[0] = solved + along * residue + next_len * (residue - step_len * image)
    for copy in sends:
        copy.wait_send()
    arrive(row_copies)
    back = collect(in_rows)
    back_high, back_low = split(back)
    back_rest = (back - back_high.astype(F32) - back_low.astype(F32)).astype(BF16)
    picked = dot(jnp.concatenate([back_high, back_low, back_rest], axis=0), select.astype(BF16))
    stress_ref[...] = (picked[:16] + (picked[16:32] + picked[32:]))[:comps]
    for copy in row_copies:
        copy.wait_send()


def place(stress_ref, field_ref, stress_out, field_out, sem):
    first = pltpu.make_async_copy(field_ref, field_out, sem.at[0])
    second = pltpu.make_async_copy(stress_ref, stress_out, sem.at[1])
    first.start()
    second.start()
    first.wait()
    second.wait()


def solution(mesh):
    groups, parts = mesh.shape["macro"], mesh.shape["rve"]

    def shards(deform, plastic, route, stiff, cubic, coupling, conn, iface, load_map, average_map):
        comps, points = deform.shape
        blocks, block = coupling.shape[1], coupling.shape[3]
        dofs = blocks * block
        capacity = 2 * points // groups
        columns = groups * capacity
        base_rows = -(-(2 * comps + 1) // 8) * 8
        vmem = pl.BlockSpec(memory_space=pltpu.VMEM)
        hbm = pl.BlockSpec(memory_space=pltpu.HBM)
        dma = pltpu.SemaphoreType.DMA
        stress, field = pl.pallas_call(
            functools.partial(kernel, groups, parts, capacity),
            out_shape=(
                pltpu.VMEM((comps, points), F32),
                pltpu.VMEM((1, dofs, columns), F32),
            ),
            in_specs=[hbm] * 6 + [pl.BlockSpec(memory_space=pltpu.SMEM)] + [hbm] * 3,
            out_specs=(vmem, vmem),
            scratch_shapes=[
                pltpu.VMEM(deform.shape, F32),
                pltpu.VMEM((1, points), jnp.int32),
                pltpu.VMEM((1, points), jnp.int32),
                pltpu.VMEM((1, dofs), F32),
                pltpu.VMEM((1, dofs), F32),
                pltpu.VMEM(coupling.shape, F32),
                pltpu.VMEM(iface.shape, F32),
                pltpu.VMEM((comps, 1, dofs), F32),
                pltpu.VMEM((comps, 1, dofs), F32),
                pltpu.VMEM((dofs, dofs), F32),
                pltpu.VMEM((dofs + 16 + block, dofs + 2 * block), BF16),
                pltpu.VMEM((dofs + 16 + block, dofs + 2 * block), BF16),
                pltpu.VMEM((16, columns), F32),
                pltpu.VMEM((groups, 16, columns), F32),
                pltpu.VMEM((40 + block // 2, LANES), F32),
                pltpu.VMEM((40, LANES), F32),
                pltpu.VMEM((40 + block // 2, LANES), F32),
                pltpu.VMEM((base_rows, dofs), F32),
                pltpu.VMEM((base_rows, dofs), F32),
                pltpu.VMEM((block, dofs), F32),
                pltpu.VMEM((16, dofs + LANES), F32),
                pltpu.VMEM((16, dofs + LANES), F32),
                pltpu.VMEM((16, LANES), F32),
                pltpu.VMEM((16, LANES), F32),
                pltpu.VMEM((parts, 16, LANES), F32),
                pltpu.VMEM((parts, -(-(6 + 2 * comps) // 8) * 8, columns), F32),
                pltpu.VMEM((16, columns), F32),
                pltpu.VMEM((groups, 16, columns), F32),
                dma((9,)),
                dma((groups - 1,)), dma((groups - 1,)),
                dma((2,)), dma((2,)),
                dma((4,)), dma((4,)),
                dma((parts - 1,)), dma((parts - 1,)),
                dma((parts - 1,)), dma((parts - 1,)),
                dma((groups - 1,)), dma((groups - 1,)),
            ],
            compiler_params=pltpu.CompilerParams(
                collective_id=0, has_side_effects=True, vmem_limit_bytes=60 * 1024 * 1024
            ),
        )(
            deform, plastic[None], route[None], stiff, cubic, coupling,
            jnp.transpose(conn, (0, 2, 1)), iface,
            jnp.transpose(load_map, (1, 0, 2)), jnp.transpose(average_map, (1, 0, 2)),
        )
        return pl.pallas_call(
            place,
            out_shape=(
                jax.ShapeDtypeStruct((comps, points), F32),
                jax.ShapeDtypeStruct((1, dofs, columns), F32),
            ),
            in_specs=[vmem, vmem], out_specs=(hbm, hbm),
            scratch_shapes=[dma((2,))],
        )(*(pltpu.with_memory_space_constraint(x, pltpu.VMEM) for x in (stress, field)))

    return jax.shard_map(
        shards,
        mesh=mesh,
        in_specs=(
            P(None, "macro"),
            P("macro"),
            P("macro"),
            P("macro", "rve"),
            P("macro", "rve"),
            P("macro", "rve", None, None, None),
            P("macro", "rve", None),
            P("macro", "rve", None),
            P("macro", None, "rve"),
            P("macro", None, "rve"),
        ),
        out_specs=(P(None, "macro"), P("macro", "rve", None)),
        check_vma=False,
    )
```

```python
import functools

import jax
import jax.numpy as jnp
from jax import lax
from jax.experimental import pallas as pl
from jax.experimental.pallas import tpu as pltpu
from jax.sharding import PartitionSpec as P

EPSILON = 1e-06
SCALE = 2.0 ** -20
MESH = pl.DeviceIdType.MESH
HIGHEST = lax.Precision.HIGHEST
F32 = jnp.float32
BF16 = jnp.bfloat16
LANES = 128
NT = (((1,), (1,)), ((), ()))


def split(values):
    high = values.astype(BF16)
    return high, (values - high.astype(F32)).astype(BF16)


def dot(left, right):
    return jnp.dot(left, right, preferred_element_type=F32)


def dot_nt(left, right, precision=None):
    return lax.dot_general(left, right, NT, precision=precision, preferred_element_type=F32)


def apply_split(high, low, values):
    value_high, value_low = split(values)
    width = values.shape[1]
    wide = dot(high, jnp.concatenate([value_high, value_low], axis=1))
    return wide[:, :width] + wide[:, width:] + dot(low, value_high)


def apply_rows(values, high, low):
    value_high, value_low = split(values)
    rows = values.shape[0]
    tall = dot(jnp.concatenate([value_high, value_low], axis=0), high)
    return tall[:rows] + tall[rows:] + dot(value_high, low)


def dot_nt_split(left, right):
    left_high, left_low = split(left)
    right_high, right_low = split(right)
    rows = left.shape[0]
    tall = dot_nt(jnp.concatenate([left_high, left_low], axis=0), right_high)
    return tall[:rows] + tall[rows:] + dot_nt(left_high, right_low)


def square_nt(values):
    high, low = split(values)
    return dot_nt(high, high) + (dot_nt(high, low) + dot_nt(low, high))


def iota(shape, dim):
    return lax.broadcasted_iota(jnp.int32, shape, dim)


def pad_rows(values, rows):
    missing = rows - values.shape[0]
    if missing == 0:
        return values
    return jnp.concatenate([values, jnp.zeros((missing, values.shape[1]), values.dtype)], axis=0)


def col_sum(values):
    return jnp.sum(values, axis=0, keepdims=True)


def kernel(
    groups, parts, capacity,
    deform_hbm, plastic_hbm, route_hbm, stiff_hbm, cubic_hbm, coupling_hbm, conn_ref,
    iface_hbm, load_hbm, average_hbm,
    stress_ref, field_ref,
    deform_ref, plastic_ref, route_ref, stiff_ref, cubic_ref, coupling_ref,
    iface_ref, load_ref, average_ref,
    whole, stiff_high, stiff_low,
    out_points, in_points, edge_out, prev_in, next_in,
    base_out, base_in, last_in, map_out, map_in, head_out, head_in,
    gram_buf, sum_out, sum_buf, twin_buf, mean_out, mean_in, out_rows, in_rows,
    input_sem,
    point_send, point_recv, edge_send, edge_recv, ghost_send, ghost_recv,
    gram_send, gram_recv, sum_send, sum_recv, twin_send, twin_recv, row_send, row_recv,
):
    group = lax.axis_index("macro")
    part = lax.axis_index("rve")
    twin = group + 1 - 2 * lax.rem(group, 2)
    blocks, slots, block = coupling_ref.shape[1], coupling_ref.shape[2], coupling_ref.shape[3]
    dofs = blocks * block
    comps, points = deform_ref.shape
    columns = groups * capacity

    barrier = pltpu.get_barrier_semaphore()
    for step in range(1, parts):
        pl.semaphore_signal(
            barrier, inc=1, device_id={"rve": lax.rem(part + step, parts)}, device_id_type=MESH
        )
    for step in range(1, groups):
        pl.semaphore_signal(
            barrier, inc=1, device_id={"macro": lax.rem(group + step, groups)}, device_id_type=MESH
        )

    loads = []
    for source, target in (
        (coupling_hbm, coupling_ref), (iface_hbm, iface_ref), (load_hbm, load_ref),
        (cubic_hbm, cubic_ref), (stiff_hbm, stiff_ref), (deform_hbm, deform_ref),
        (plastic_hbm, plastic_ref), (route_hbm, route_ref), (average_hbm, average_ref),
    ):
        loads.append(pltpu.make_async_copy(source, target, input_sem.at[len(loads)]))
        loads[-1].start()
    coupling_load, iface_load = loads[:2]
    early_loads, late_loads = loads[2:5], loads[5:]

    def exchange(source, target, place, send, recv):
        copies = []
        for step in range(1, groups):
            copies.append(pltpu.make_async_remote_copy(
                src_ref=source, dst_ref=target.at[place],
                send_sem=send.at[step - 1], recv_sem=recv.at[step - 1],
                device_id={"macro": lax.rem(group + step, groups)}, device_id_type=MESH,
            ))
            copies[-1].start()
        return copies

    def collect(buffer):
        owner = iota((16, columns), 1) // capacity
        found = jnp.zeros((16, columns), F32)
        for other in range(groups):
            shift = lax.rem(other + groups - group, groups) * capacity
            found = jnp.where(owner == other, pltpu.roll(buffer[other], shift, 1), found)
        return found

    def share(buffer, send, recv):
        copies = []
        for step in range(1, parts):
            copies.append(pltpu.make_async_remote_copy(
                src_ref=buffer.at[part], dst_ref=buffer.at[part],
                send_sem=send.at[step - 1], recv_sem=recv.at[step - 1],
                device_id={"rve": lax.rem(part + step, parts)}, device_id_type=MESH,
            ))
            copies[-1].start()
        return copies

    after, behind = lax.rem(part + 1, parts), lax.rem(part + parts - 1, parts)

    def push(source, target, peer, send, recv, place):
        copy = pltpu.make_async_remote_copy(
            src_ref=source, dst_ref=target, send_sem=send.at[place], recv_sem=recv.at[place],
            device_id={"rve": peer}, device_id_type=MESH,
        )
        copy.start()
        return copy

    def hand_over(source, target, peer, place):
        copy = pltpu.make_async_remote_copy(
            src_ref=source, dst_ref=target, send_sem=twin_send.at[place], recv_sem=twin_recv.at[place],
            device_id={"macro": twin, "rve": peer}, device_id_type=MESH,
        )
        copy.start()
        return copy

    def arrive(copies):
        for copy in copies:
            copy.wait_recv()

    def gathered(buffer):
        total = buffer[0]
        for other in range(1, parts):
            total = total + buffer[other]
        return total

    coupling_load.wait()
    lane = iota((block, LANES), 1) < block
    doubled = []
    for row in range(blocks):
        square = square_nt(coupling_ref[0, row].reshape(slots * block, block))
        doubled.append([])
        for slot in range(slots):
            spring = square[slot * block:(slot + 1) * block, slot * block:(slot + 1) * block]
            doubled[row].append(jnp.concatenate([spring, spring], axis=1))

    def mark(row, slot, far):
        if row == far:
            return jnp.float32(0.0)
        return jnp.where(conn_ref[0, slot, row] == far, 1.0, 0.0).astype(F32)

    for row in range(blocks):
        own = doubled[row][0]
        for slot in range(1, slots):
            own = own + doubled[row][slot]
        for other in range(blocks):
            if other != row:
                for slot in range(slots):
                    own = own + doubled[other][slot] * mark(other, slot, row)
        for pair in range(blocks // 2):
            left, right = 2 * pair, 2 * pair + 1
            value = jnp.zeros((block, LANES), F32)
            for slot in range(slots):
                value = value - doubled[row][slot] * jnp.where(
                    lane, mark(row, slot, left), mark(row, slot, right)
                )
                value = value - jnp.where(
                    lane, doubled[left][slot] * mark(left, slot, row),
                    doubled[right][slot] * mark(right, slot, row),
                )
            if row == left:
                value = value + jnp.where(lane, own, 0.0)
            if row == right:
                value = value + jnp.where(lane, 0.0, own)
            whole[row * block:(row + 1) * block, pair * LANES:(pair + 1) * LANES] = value

    iface_load.wait()
    for copy in early_loads:
        copy.wait()
    own_edge = iface_ref[0]
    own_spring = square_nt(own_edge)
    own_high, own_low = split(own_spring)
    diagonal = iota((dofs, dofs), 0) == iota((dofs, dofs), 1)
    stiffness = whole[...] + jnp.where(diagonal, stiff_ref[...], 0.0)
    high, low = split(stiffness)
    stiff_high[:dofs, :dofs] = high
    stiff_low[:dofs, :dofs] = low
    whole[dofs - block:, :] = stiffness[dofs - block:, :]
    high, low = split(stiffness[:block, :block] + own_spring)
    stiff_high[:block, :block] = high
    stiff_low[:block, :block] = low
    for target, spring in ((stiff_high, own_high), (stiff_low, own_low)):
        target[:dofs, dofs:] = jnp.zeros((dofs, 2 * block), BF16)
        target[dofs:, :] = jnp.zeros((16 + block, dofs + 2 * block), BF16)
        target[:block, dofs:dofs + block] = -spring
        target[dofs + 16:, :block] = spring

    maps = pad_rows(load_ref[:, 0, :], 16)
    cubic = pad_rows(cubic_ref[...], 16)

    def ends(values):
        return jnp.concatenate([values[:, :block], values[:, dofs - block:]], axis=1)

    image_map = apply_rows(maps, stiff_high[:dofs, :dofs], stiff_low[:dofs, :dofs])
    base_out[...] = pad_rows(
        jnp.concatenate([maps[:comps], image_map[:comps], cubic[:1]], axis=0), base_out.shape[0]
    )
    edge_out[:40, :] = ends(jnp.concatenate([maps, image_map, cubic[:8]], axis=0))
    edge_out[40:, :] = jnp.concatenate([own_edge[:block // 2], own_edge[block // 2:]], axis=1)

    pl.semaphore_wait(barrier, groups + parts - 2)

    sends = []
    edge_copies = [
        push(edge_out.at[pl.ds(0, 40)], prev_in, after, edge_send, edge_recv, 0),
        push(edge_out, next_in, behind, edge_send, edge_recv, 1),
    ]

    ghost_copies = [
        push(base_out, base_in, after, ghost_send, ghost_recv, 0),
        push(whole.at[pl.ds(dofs - block, block)], last_in, after, ghost_send, ghost_recv, 1),
    ]

    for copy in late_loads:
        copy.wait()
    route = route_ref[...]
    hot = (iota((groups, points), 0) == route).astype(F32)
    before = (iota((points, points), 0) < iota((points, points), 1)).astype(BF16)
    rank = col_sum(hot * dot(hot.astype(BF16), before))
    slot_of = (route * capacity).astype(F32) + rank
    select = (iota((columns, points), 0).astype(F32) == slot_of).astype(F32)
    sent = pad_rows(
        jnp.concatenate([deform_ref[...], plastic_ref[...].astype(F32)], axis=0), 16
    )
    out_points[...] = dot_nt(sent, select, HIGHEST)
    point_copies = exchange(out_points, in_points, group, point_send, point_recv)
    sends += point_copies + edge_copies + ghost_copies
    in_points[group] = out_points[...]
    averages = pad_rows(average_ref[:, 0, :], 16)
    average_high, average_low = split(averages)
    stiff_high[dofs:dofs + 16, :dofs] = average_high
    stiff_low[dofs:dofs + 16, :dofs] = average_low

    def own_rows(values):
        return apply_rows(values, own_high, own_low)

    def next_rows(values):
        return apply_rows(values, next_high, next_low)

    def unpack(values):
        return jnp.concatenate([
            pad_rows(values[:comps], 16), pad_rows(values[comps:2 * comps], 16),
            pad_rows(values[2 * comps:2 * comps + 1], 16),
        ], axis=0)

    first_map, last_map = maps[:, :block], maps[:, dofs - block:]
    through_first = own_rows(first_map)
    second_map = apply_rows(image_map, stiff_high[:dofs, :dofs], stiff_low[:dofs, :dofs])
    ends_high = jnp.concatenate([stiff_high[:block, :dofs], stiff_high[dofs - block:dofs, :dofs]], axis=0)
    ends_low = jnp.concatenate([stiff_low[:block, :dofs], stiff_low[dofs - block:dofs, :dofs]], axis=0)

    arrive(edge_copies)
    packed = next_in[40:, :]
    next_spring = square_nt(jnp.concatenate([packed[:, :block], packed[:, block:]], axis=0))
    next_high, next_low = split(next_spring)
    prev_map, next_map = prev_in[0:16, block:], next_in[0:16, :block]
    through_prev = own_rows(prev_map)
    through_next = next_rows(jnp.concatenate([last_map - next_map, last_map], axis=0))
    prev_image = prev_in[16:32, block:] + through_prev - through_first
    next_image = next_in[16:32, :block] - through_next[16:]
    change = jnp.concatenate([-through_prev, through_next[:16]], axis=1)
    image_map = jnp.concatenate([
        image_map[:, :block] + change[:, :block],
        image_map[:, block:dofs - block],
        image_map[:, dofs - block:] + change[:, block:],
    ], axis=1)
    second_map = second_map + apply_rows(change, ends_high, ends_low)
    second_map = jnp.concatenate([
        second_map[:, :block] - own_rows(prev_image),
        second_map[:, block:dofs - block],
        second_map[:, dofs - block:] + next_rows(image_map[:, dofs - block:] - next_image),
    ], axis=1)
    products = dot_nt_split(
        jnp.concatenate([maps, image_map, averages], axis=0),
        jnp.concatenate([maps, image_map, second_map], axis=0),
    )
    gram_buf[part] = jnp.concatenate([
        products[0:16, 0:32], products[16:32, 16:48], products[32:48], jnp.zeros((16, 16), F32),
    ], axis=1)
    map_out[:, :dofs] = second_map
    map_out[:, dofs:] = jnp.concatenate([image_map[:, :block], jnp.zeros((16, block), F32)], axis=1)
    head_out[...] = second_map[:, :LANES]
    gram_copies = share(gram_buf, gram_send, gram_recv)
    map_copies = [
        push(map_out, map_in, after, ghost_send, ghost_recv, 2),
        push(head_out, head_in, behind, ghost_send, ghost_recv, 3),
    ]
    sends += map_copies + gram_copies
    high, low = split(stiffness[dofs - block:, dofs - block:] + next_spring)
    stiff_high[dofs - block:dofs, dofs - block:dofs] = high
    stiff_low[dofs - block:dofs, dofs - block:dofs] = low
    stiff_high[dofs - block:dofs, dofs + block:] = -next_high
    stiff_low[dofs - block:dofs, dofs + block:] = -next_low

    def early_cols(map_rows, image_rows, cubic_rows):
        map_high, map_low = split(map_rows)
        image_high, image_low = split(image_rows)
        both_high = jnp.concatenate([map_high, image_high], axis=0).astype(F32)
        both_low = jnp.concatenate([map_low, image_low], axis=0).astype(F32)
        rows = jnp.concatenate([both_high, both_high, both_low, pad_rows(cubic_rows, 32)], axis=0)
        cols = jnp.transpose(rows)
        return cols.astype(BF16), cols[:, 96:97]

    def late_cols(second_rows, image_rows):
        second_high, second_low = split(second_rows)
        image_high, image_low = split(image_rows)
        return jnp.transpose(jnp.concatenate([
            second_high, second_high, second_low, image_high, image_high, image_low,
            jnp.zeros((32, second_rows.shape[1]), BF16),
        ], axis=0))

    own_early, own_cubic = early_cols(maps, image_map, cubic)
    own_late = late_cols(second_map, jnp.zeros_like(second_map))
    arrive(point_copies)
    received = collect(in_points)
    flag = received[comps:comps + 1]
    strain = jnp.where(iota((16, columns), 0) < comps, received, 0.0)
    strain_high, strain_low = split(strain)
    hard = own_cubic * flag

    arrive(ghost_copies)
    prev_rows = unpack(base_in[...])
    last_rows = last_in[...]
    last_high, last_low = split(jnp.concatenate([
        last_rows[:, :dofs - LANES],
        last_rows[:, dofs - LANES:] + jnp.concatenate([jnp.zeros_like(own_spring), own_spring], axis=1),
    ], axis=1))
    ghost_early, ghost_cubic = early_cols(
        jnp.concatenate([prev_rows[0:16], next_map], axis=1),
        jnp.concatenate([
            jnp.zeros((16, block), F32), prev_rows[16:32, block:dofs - block], prev_image, next_image,
        ], axis=1),
        jnp.concatenate([prev_rows[32:40], next_in[32:40, :block]], axis=1),
    )
    ghost_hard = ghost_cubic * flag

    arrive(gram_copies)
    gram = gathered(gram_buf)
    form_high, form_low = split(jnp.concatenate(
        [gram[:, 0:16], gram[:, 16:32], gram[:, 32:48], gram[:, 48:64]], axis=0
    ))
    wide = dot(
        jnp.concatenate([form_high, form_low], axis=0), jnp.concatenate([strain_high, strain_low], axis=1)
    )
    forms = wide[:64, :columns] + (wide[:64, columns:] + wide[64:, :columns])
    norm = col_sum(forms[0:16] * strain)
    curve = col_sum(forms[16:32] * strain)
    third = col_sum(forms[32:48] * strain)
    fourth = col_sum(forms[48:64] * strain)

    def second_step(norm, curve, left_norm, left_curve, cross):
        ratio = left_norm / (norm + EPSILON)
        next_curve = left_curve + ratio * (2.0 * cross + ratio * curve)
        next_curve = jnp.maximum(next_curve, 0.09 * left_norm)
        next_len = left_norm / (next_curve + EPSILON)
        return next_len, next_len * ratio

    step_len = norm / (curve + EPSILON)
    left_norm = jnp.maximum(norm - step_len * (2.0 * curve - step_len * third), 0.0)
    left_curve = curve - step_len * (2.0 * third - step_len * fourth)
    cross = curve - step_len * third
    next_len, carried = second_step(norm, curve, left_norm, left_curve, cross)
    along = step_len + carried + next_len
    across = next_len * step_len
    weights = jnp.concatenate([
        jnp.concatenate([along * strain, -across * strain, jnp.zeros_like(strain)], axis=0),
        jnp.concatenate([strain, -along * strain, across * strain], axis=0),
    ], axis=1)
    weight_high, weight_low = split(weights)
    arrive(map_copies)
    ghost_late = late_cols(
        jnp.concatenate([map_in[:, :dofs], head_in[:, :block]], axis=1),
        jnp.concatenate([map_in[:, dofs:dofs + block], jnp.zeros((16, dofs), F32)], axis=1),
    )
    blank = jnp.zeros((32, 2 * columns), BF16)
    both = dot(
        jnp.concatenate([
            jnp.concatenate([own_early, own_late], axis=1), jnp.concatenate([ghost_early, ghost_late], axis=1),
        ], axis=0),
        jnp.concatenate([
            weight_high[:32], weight_low[:32], weight_high[:32], blank,
            weight_high[32:], weight_low[32:], weight_high[32:],
            weight_high[16:32], weight_low[16:32], weight_high[16:32], blank,
        ], axis=0),
    )
    solved = both[:dofs, :columns]
    hard_square = hard * solved * solved
    tangent = 3.0 * hard_square
    residue = both[:dofs, columns:] - hard_square * solved
    ghost_solved = both[dofs:, :columns]
    ghost_square = ghost_hard * ghost_solved * ghost_solved
    ghost = both[dofs:, columns:] - ghost_square * ghost_solved
    own_product = apply_split(
        stiff_high[...], stiff_low[...], jnp.concatenate([residue, ghost[dofs - block:]], axis=0)
    )
    last_product = apply_split(last_high, last_low, ghost[:dofs])
    image = own_product[:dofs] + tangent * residue
    last_residue = ghost[dofs - block:dofs]
    last_image = (
        last_product + 3.0 * ghost_square[dofs - block:dofs] * last_residue - own_product[dofs + 16:]
    )
    image_product = apply_split(
        stiff_high[...], stiff_low[...],
        jnp.concatenate([image, 2.0 * last_image, jnp.zeros_like(last_image)], axis=0),
    )

    mean_out[...] = jnp.dot(
        gram[:, 64:112], weights[:, :columns], precision=HIGHEST, preferred_element_type=F32
    )
    mean_copy = hand_over(mean_out, mean_in, part, parts)

    scaled = SCALE * image
    length = jnp.sqrt(col_sum(scaled * scaled))
    inverse = jnp.where(length > 0.0, SCALE / jnp.where(length > 0.0, length, 1.0), 0.0)
    length = length * (1.0 / SCALE)
    unit = inverse * image
    along_unit = col_sum(residue * unit)
    rest = residue - along_unit * unit
    form_unit = inverse * (image_product[:dofs] + tangent * image)
    form_rest = jnp.concatenate([
        image[:block] - apply_split(own_high, own_low, last_residue), image[block:dofs - block],
        image[dofs - block:] + apply_split(next_high, next_low, ghost[dofs:]),
    ], axis=0) - along_unit * form_unit
    sum_out[...] = pad_rows(jnp.concatenate([
        length, along_unit, col_sum(rest * rest),
        col_sum(rest * form_rest), col_sum(rest * form_unit + unit * form_rest), col_sum(unit * form_unit),
        own_product[dofs:dofs + comps], image_product[dofs:dofs + comps],
    ], axis=0), sum_out.shape[0])
    twin_copies = [mean_copy]
    for step in range(parts):
        peer = lax.rem(part + step, parts)
        twin_copies.append(hand_over(sum_out, twin_buf.at[part], peer, step))
    sum_buf[part] = sum_out[:8]
    sum_copies = share(sum_buf, sum_send, sum_recv)
    sends += sum_copies + twin_copies
    def lengths(sums):
        norm = sum(each[2:3] + each[1:2] * each[1:2] for each in sums)
        curve = sum(each[0:1] * each[1:2] for each in sums)
        step_len = norm / (curve + EPSILON)
        left_norm, left_curve, cross = 0.0, 0.0, 0.0
        for each in sums:
            beyond = step_len * each[0:1] - each[1:2]
            left_norm = left_norm + (each[2:3] + beyond * beyond)
            left_curve = left_curve + (each[3:4] - beyond * (each[4:5] - beyond * each[5:6]))
            cross = cross - beyond * each[0:1]
        next_len, carried = second_step(norm, curve, left_norm, left_curve, cross)
        return step_len, next_len, step_len + carried

    arrive(twin_copies)
    sums = [twin_buf[other] for other in range(parts)]
    means = sum(sums[1:], sums[0])[6:]
    step_len, next_len, along = lengths(sums)
    total = (
        mean_in[:comps] + along * means[:comps]
        + next_len * (means[:comps] - step_len * means[comps:2 * comps])
    )

    out_rows[...] = pad_rows(total, 16)
    row_copies = exchange(out_rows, in_rows, twin, row_send, row_recv)
    in_rows[twin] = out_rows[...]
    arrive(sum_copies)
    step_len, next_len, along = lengths([sum_buf[other] for other in range(parts)])
    field_ref[0] = solved + along * residue + next_len * (residue - step_len * image)
    for copy in sends:
        copy.wait_send()
    arrive(row_copies)
    back = collect(in_rows)
    back_high, back_low = split(back)
    back_rest = (back - back_high.astype(F32) - back_low.astype(F32)).astype(BF16)
    picked = dot(jnp.concatenate([back_high, back_low, back_rest], axis=0), select.astype(BF16))
    stress_ref[...] = (picked[:16] + (picked[16:32] + picked[32:]))[:comps]
    for copy in row_copies:
        copy.wait_send()


def place(stress_ref, field_ref, stress_out, field_out, sem):
    first = pltpu.make_async_copy(field_ref, field_out, sem.at[0])
    second = pltpu.make_async_copy(stress_ref, stress_out, sem.at[1])
    first.start()
    second.start()
    first.wait()
    second.wait()


def solution(mesh):
    groups, parts = mesh.shape["macro"], mesh.shape["rve"]

    def shards(deform, plastic, route, stiff, cubic, coupling, conn, iface, load_map, average_map):
        comps, points = deform.shape
        blocks, block = coupling.shape[1], coupling.shape[3]
        dofs = blocks * block
        capacity = 2 * points // groups
        columns = groups * capacity
        sum_rows = -(-(6 + 2 * comps) // 8) * 8
        base_rows = -(-(2 * comps + 1) // 8) * 8
        vmem = pl.BlockSpec(memory_space=pltpu.VMEM)
        hbm = pl.BlockSpec(memory_space=pltpu.HBM)
        dma = pltpu.SemaphoreType.DMA
        stress, field = pl.pallas_call(
            functools.partial(kernel, groups, parts, capacity),
            out_shape=(
                pltpu.VMEM((comps, points), F32),
                pltpu.VMEM((1, dofs, columns), F32),
            ),
            in_specs=[hbm] * 6 + [pl.BlockSpec(memory_space=pltpu.SMEM)] + [hbm] * 3,
            out_specs=(vmem, vmem),
            scratch_shapes=[
                pltpu.VMEM(deform.shape, F32),
                pltpu.VMEM((1, points), jnp.int32),
                pltpu.VMEM((1, points), jnp.int32),
                pltpu.VMEM((1, dofs), F32),
                pltpu.VMEM((1, dofs), F32),
                pltpu.VMEM(coupling.shape, F32),
                pltpu.VMEM(iface.shape, F32),
                pltpu.VMEM((comps, 1, dofs), F32),
                pltpu.VMEM((comps, 1, dofs), F32),
                pltpu.VMEM((dofs, dofs), F32),
                pltpu.VMEM((dofs + 16 + block, dofs + 2 * block), BF16),
                pltpu.VMEM((dofs + 16 + block, dofs + 2 * block), BF16),
                pltpu.VMEM((16, columns), F32),
                pltpu.VMEM((groups, 16, columns), F32),
                pltpu.VMEM((40 + block // 2, LANES), F32),
                pltpu.VMEM((40, LANES), F32),
                pltpu.VMEM((40 + block // 2, LANES), F32),
                pltpu.VMEM((base_rows, dofs), F32),
                pltpu.VMEM((base_rows, dofs), F32),
                pltpu.VMEM((block, dofs), F32),
                pltpu.VMEM((16, dofs + LANES), F32),
                pltpu.VMEM((16, dofs + LANES), F32),
                pltpu.VMEM((16, LANES), F32),
                pltpu.VMEM((16, LANES), F32),
                pltpu.VMEM((parts, 16, LANES), F32),
                pltpu.VMEM((sum_rows, columns), F32),
                pltpu.VMEM((parts, 8, columns), F32),
                pltpu.VMEM((parts, sum_rows, columns), F32),
                pltpu.VMEM((16, columns), F32),
                pltpu.VMEM((16, columns), F32),
                pltpu.VMEM((16, columns), F32),
                pltpu.VMEM((groups, 16, columns), F32),
                dma((9,)),
                dma((groups - 1,)), dma((groups - 1,)),
                dma((2,)), dma((2,)),
                dma((4,)), dma((4,)),
                dma((parts - 1,)), dma((parts - 1,)),
                dma((parts - 1,)), dma((parts - 1,)),
                dma((parts + 1,)), dma((parts + 1,)),
                dma((groups - 1,)), dma((groups - 1,)),
            ],
            compiler_params=pltpu.CompilerParams(
                collective_id=0, has_side_effects=True, vmem_limit_bytes=60 * 1024 * 1024
            ),
        )(
            deform, plastic[None], route[None], stiff, cubic, coupling,
            jnp.transpose(conn, (0, 2, 1)), iface,
            jnp.transpose(load_map, (1, 0, 2)), jnp.transpose(average_map, (1, 0, 2)),
        )
        return pl.pallas_call(
            place,
            out_shape=(
                jax.ShapeDtypeStruct((comps, points), F32),
                jax.ShapeDtypeStruct((1, dofs, columns), F32),
            ),
            in_specs=[vmem, vmem], out_specs=(hbm, hbm),
            scratch_shapes=[dma((2,))],
        )(*(pltpu.with_memory_space_constraint(x, pltpu.VMEM) for x in (stress, field)))

    return jax.shard_map(
        shards,
        mesh=mesh,
        in_specs=(
            P(None, "macro"),
            P("macro"),
            P("macro"),
            P("macro", "rve"),
            P("macro", "rve"),
            P("macro", "rve", None, None, None),
            P("macro", "rve", None),
            P("macro", "rve", None),
            P("macro", None, "rve"),
            P("macro", None, "rve"),
        ),
        out_specs=(P(None, "macro"), P("macro", "rve", None)),
        check_vma=False,
    )
```

```python
import functools

import jax
import jax.numpy as jnp
from jax import lax
from jax.experimental import pallas as pl
from jax.experimental.pallas import tpu as pltpu
from jax.sharding import PartitionSpec as P

EPSILON = 1e-06
SCALE = 2.0 ** -20
MESH = pl.DeviceIdType.MESH
HIGHEST = lax.Precision.HIGHEST
F32 = jnp.float32
BF16 = jnp.bfloat16
LANES = 128
NT = (((1,), (1,)), ((), ()))


def split(values):
    high = values.astype(BF16)
    return high, (values - high.astype(F32)).astype(BF16)


def dot(left, right):
    return jnp.dot(left, right, preferred_element_type=F32)


def dot_nt(left, right, precision=None):
    return lax.dot_general(left, right, NT, precision=precision, preferred_element_type=F32)


def apply_split(high, low, values):
    value_high, value_low = split(values)
    width = values.shape[1]
    wide = dot(high, jnp.concatenate([value_high, value_low], axis=1))
    return wide[:, :width] + wide[:, width:] + dot(low, value_high)


def apply_rows(values, high, low):
    value_high, value_low = split(values)
    rows = values.shape[0]
    tall = dot(jnp.concatenate([value_high, value_low], axis=0), high)
    return tall[:rows] + tall[rows:] + dot(value_high, low)


def dot_nt_split(left, right):
    left_high, left_low = split(left)
    right_high, right_low = split(right)
    rows = left.shape[0]
    tall = dot_nt(jnp.concatenate([left_high, left_low], axis=0), right_high)
    return tall[:rows] + tall[rows:] + dot_nt(left_high, right_low)


def square_nt(values):
    high, low = split(values)
    return dot_nt(high, high) + (dot_nt(high, low) + dot_nt(low, high))


def iota(shape, dim):
    return lax.broadcasted_iota(jnp.int32, shape, dim)


def pad_rows(values, rows):
    missing = rows - values.shape[0]
    if missing == 0:
        return values
    return jnp.concatenate([values, jnp.zeros((missing, values.shape[1]), values.dtype)], axis=0)


def col_sum(values):
    return jnp.sum(values, axis=0, keepdims=True)


def kernel(
    groups, parts, capacity,
    deform_hbm, plastic_hbm, route_hbm, stiff_hbm, cubic_hbm, coupling_hbm, conn_ref,
    iface_hbm, load_hbm, average_hbm,
    stress_ref, field_ref,
    deform_ref, plastic_ref, route_ref, stiff_ref, cubic_ref, coupling_ref,
    iface_ref, load_ref, average_ref,
    whole, stiff_high, stiff_low,
    out_points, in_points, edge_out, prev_in, next_in,
    base_out, base_in, last_in, map_out, map_in, head_out, head_in,
    gram_buf, sum_out, sum_buf, twin_buf, mean_out, mean_in, out_rows, in_rows,
    input_sem,
    point_send, point_recv, edge_send, edge_recv, ghost_send, ghost_recv,
    gram_send, gram_recv, sum_send, sum_recv, twin_send, twin_recv, row_send, row_recv,
):
    group = lax.axis_index("macro")
    part = lax.axis_index("rve")
    twin = group + 1 - 2 * lax.rem(group, 2)
    blocks, slots, block = coupling_ref.shape[1], coupling_ref.shape[2], coupling_ref.shape[3]
    dofs = blocks * block
    comps, points = deform_ref.shape
    columns = groups * capacity

    barrier = pltpu.get_barrier_semaphore()
    for step in range(1, parts):
        pl.semaphore_signal(
            barrier, inc=1, device_id={"rve": lax.rem(part + step, parts)}, device_id_type=MESH
        )
    for step in range(1, groups):
        pl.semaphore_signal(
            barrier, inc=1, device_id={"macro": lax.rem(group + step, groups)}, device_id_type=MESH
        )

    loads = []
    for source, target in (
        (coupling_hbm, coupling_ref), (iface_hbm, iface_ref), (load_hbm, load_ref),
        (cubic_hbm, cubic_ref), (stiff_hbm, stiff_ref), (deform_hbm, deform_ref),
        (plastic_hbm, plastic_ref), (route_hbm, route_ref), (average_hbm, average_ref),
    ):
        loads.append(pltpu.make_async_copy(source, target, input_sem.at[len(loads)]))
        loads[-1].start()
    coupling_load, iface_load = loads[:2]
    early_loads, late_loads = loads[2:5], loads[5:]

    def exchange(source, target, place, send, recv):
        copies = []
        for step in range(1, groups):
            copies.append(pltpu.make_async_remote_copy(
                src_ref=source, dst_ref=target.at[place],
                send_sem=send.at[step - 1], recv_sem=recv.at[step - 1],
                device_id={"macro": lax.rem(group + step, groups)}, device_id_type=MESH,
            ))
            copies[-1].start()
        return copies

    def collect(buffer):
        owner = iota((16, columns), 1) // capacity
        found = jnp.zeros((16, columns), F32)
        for other in range(groups):
            shift = lax.rem(other + groups - group, groups) * capacity
            found = jnp.where(owner == other, pltpu.roll(buffer[other], shift, 1), found)
        return found

    def share(buffer, send, recv):
        copies = []
        for step in range(1, parts):
            copies.append(pltpu.make_async_remote_copy(
                src_ref=buffer.at[part], dst_ref=buffer.at[part],
                send_sem=send.at[step - 1], recv_sem=recv.at[step - 1],
                device_id={"rve": lax.rem(part + step, parts)}, device_id_type=MESH,
            ))
            copies[-1].start()
        return copies

    after, behind = lax.rem(part + 1, parts), lax.rem(part + parts - 1, parts)

    def push(source, target, peer, send, recv, place):
        copy = pltpu.make_async_remote_copy(
            src_ref=source, dst_ref=target, send_sem=send.at[place], recv_sem=recv.at[place],
            device_id={"rve": peer}, device_id_type=MESH,
        )
        copy.start()
        return copy

    def hand_over(source, target, peer, place):
        copy = pltpu.make_async_remote_copy(
            src_ref=source, dst_ref=target, send_sem=twin_send.at[place], recv_sem=twin_recv.at[place],
            device_id={"macro": twin, "rve": peer}, device_id_type=MESH,
        )
        copy.start()
        return copy

    def arrive(copies):
        for copy in copies:
            copy.wait_recv()

    def gathered(buffer):
        total = buffer[0]
        for other in range(1, parts):
            total = total + buffer[other]
        return total

    coupling_load.wait()
    lane = iota((block, LANES), 1) < block
    doubled = []
    for row in range(blocks):
        square = square_nt(coupling_ref[0, row].reshape(slots * block, block))
        doubled.append([])
        for slot in range(slots):
            spring = square[slot * block:(slot + 1) * block, slot * block:(slot + 1) * block]
            doubled[row].append(jnp.concatenate([spring, spring], axis=1))

    def mark(row, slot, far):
        if row == far:
            return jnp.float32(0.0)
        return jnp.where(conn_ref[0, slot, row] == far, 1.0, 0.0).astype(F32)

    for row in range(blocks):
        own = doubled[row][0]
        for slot in range(1, slots):
            own = own + doubled[row][slot]
        for other in range(blocks):
            if other != row:
                for slot in range(slots):
                    own = own + doubled[other][slot] * mark(other, slot, row)
        for pair in range(blocks // 2):
            left, right = 2 * pair, 2 * pair + 1
            value = jnp.zeros((block, LANES), F32)
            for slot in range(slots):
                value = value - doubled[row][slot] * jnp.where(
                    lane, mark(row, slot, left), mark(row, slot, right)
                )
                value = value - jnp.where(
                    lane, doubled[left][slot] * mark(left, slot, row),
                    doubled[right][slot] * mark(right, slot, row),
                )
            if row == left:
                value = value + jnp.where(lane, own, 0.0)
            if row == right:
                value = value + jnp.where(lane, 0.0, own)
            whole[row * block:(row + 1) * block, pair * LANES:(pair + 1) * LANES] = value

    iface_load.wait()
    for copy in early_loads:
        copy.wait()
    own_spring = square_nt(iface_ref[0])
    own_high, own_low = split(own_spring)
    diagonal = iota((dofs, dofs), 0) == iota((dofs, dofs), 1)
    stiffness = whole[...] + jnp.where(diagonal, stiff_ref[...], 0.0)
    high, low = split(stiffness)
    stiff_high[:dofs, :dofs] = high
    stiff_low[:dofs, :dofs] = low
    whole[dofs - block:, :] = stiffness[dofs - block:, :]
    high, low = split(stiffness[:block, :block] + own_spring)
    stiff_high[:block, :block] = high
    stiff_low[:block, :block] = low
    for target, spring in ((stiff_high, own_high), (stiff_low, own_low)):
        target[:dofs, dofs:] = jnp.zeros((dofs, 2 * block), BF16)
        target[dofs:, :] = jnp.zeros((16 + block, dofs + 2 * block), BF16)
        target[:block, dofs:dofs + block] = -spring
        target[dofs + 16:, :block] = spring

    maps = pad_rows(load_ref[:, 0, :], 16)
    cubic = pad_rows(cubic_ref[...], 16)

    def ends(values):
        return jnp.concatenate([values[:, :block], values[:, dofs - block:]], axis=1)

    image_map = apply_rows(maps, stiff_high[:dofs, :dofs], stiff_low[:dofs, :dofs])
    base_out[...] = pad_rows(
        jnp.concatenate([maps[:comps], image_map[:comps], cubic[:1]], axis=0), base_out.shape[0]
    )
    edge_out[:40, :] = ends(jnp.concatenate([maps, image_map, cubic[:8]], axis=0))
    edge_out[40:, :] = jnp.concatenate([own_spring[:block // 2], own_spring[block // 2:]], axis=1)

    pl.semaphore_wait(barrier, groups + parts - 2)

    sends = []
    edge_copies = [
        push(edge_out.at[pl.ds(0, 40)], prev_in, after, edge_send, edge_recv, 0),
        push(edge_out, next_in, behind, edge_send, edge_recv, 1),
    ]

    ghost_copies = [
        push(base_out, base_in, after, ghost_send, ghost_recv, 0),
        push(whole.at[pl.ds(dofs - block, block)], last_in, after, ghost_send, ghost_recv, 1),
    ]

    for copy in late_loads:
        copy.wait()
    route = route_ref[...]
    hot = (iota((groups, points), 0) == route).astype(F32)
    before = (iota((points, points), 0) < iota((points, points), 1)).astype(BF16)
    rank = col_sum(hot * dot(hot.astype(BF16), before))
    slot_of = (route * capacity).astype(F32) + rank
    select = (iota((columns, points), 0).astype(F32) == slot_of).astype(F32)
    sent = pad_rows(
        jnp.concatenate([deform_ref[...], plastic_ref[...].astype(F32)], axis=0), 16
    )
    out_points[...] = dot_nt(sent, select, HIGHEST)
    point_copies = exchange(out_points, in_points, group, point_send, point_recv)
    sends += point_copies + edge_copies + ghost_copies
    in_points[group] = out_points[...]
    averages = pad_rows(average_ref[:, 0, :], 16)
    average_high, average_low = split(averages)
    stiff_high[dofs:dofs + 16, :dofs] = average_high
    stiff_low[dofs:dofs + 16, :dofs] = average_low

    def own_rows(values):
        return apply_rows(values, own_high, own_low)

    def next_rows(values):
        return apply_rows(values, next_high, next_low)

    def unpack(values):
        return jnp.concatenate([
            pad_rows(values[:comps], 16), pad_rows(values[comps:2 * comps], 16),
            pad_rows(values[2 * comps:2 * comps + 1], 16),
        ], axis=0)

    first_map, last_map = maps[:, :block], maps[:, dofs - block:]
    through_first = own_rows(first_map)
    second_map = apply_rows(image_map, stiff_high[:dofs, :dofs], stiff_low[:dofs, :dofs])
    ends_high = jnp.concatenate([stiff_high[:block, :dofs], stiff_high[dofs - block:dofs, :dofs]], axis=0)
    ends_low = jnp.concatenate([stiff_low[:block, :dofs], stiff_low[dofs - block:dofs, :dofs]], axis=0)

    arrive(edge_copies)
    packed = next_in[40:, :]
    next_spring = jnp.concatenate([packed[:, :block], packed[:, block:]], axis=0)
    next_high, next_low = split(next_spring)
    prev_map, next_map = prev_in[0:16, block:], next_in[0:16, :block]
    through_prev = own_rows(prev_map)
    through_next = next_rows(jnp.concatenate([last_map - next_map, last_map], axis=0))
    prev_image = prev_in[16:32, block:] + through_prev - through_first
    next_image = next_in[16:32, :block] - through_next[16:]
    change = jnp.concatenate([-through_prev, through_next[:16]], axis=1)
    image_map = jnp.concatenate([
        image_map[:, :block] + change[:, :block],
        image_map[:, block:dofs - block],
        image_map[:, dofs - block:] + change[:, block:],
    ], axis=1)
    second_map = second_map + apply_rows(change, ends_high, ends_low)
    second_map = jnp.concatenate([
        second_map[:, :block] - own_rows(prev_image),
        second_map[:, block:dofs - block],
        second_map[:, dofs - block:] + next_rows(image_map[:, dofs - block:] - next_image),
    ], axis=1)
    products = dot_nt_split(
        jnp.concatenate([maps, image_map, averages], axis=0),
        jnp.concatenate([maps, image_map, second_map], axis=0),
    )
    gram_buf[part] = jnp.concatenate([
        products[0:16, 0:32], products[16:32, 16:48], products[32:48], jnp.zeros((16, 16), F32),
    ], axis=1)
    map_out[:, :dofs] = second_map
    map_out[:, dofs:] = jnp.concatenate([image_map[:, :block], jnp.zeros((16, block), F32)], axis=1)
    head_out[...] = second_map[:, :LANES]
    gram_copies = share(gram_buf, gram_send, gram_recv)
    map_copies = [
        push(map_out, map_in, after, ghost_send, ghost_recv, 2),
        push(head_out, head_in, behind, ghost_send, ghost_recv, 3),
    ]
    sends += map_copies + gram_copies
    high, low = split(stiffness[dofs - block:, dofs - block:] + next_spring)
    stiff_high[dofs - block:dofs, dofs - block:dofs] = high
    stiff_low[dofs - block:dofs, dofs - block:dofs] = low
    stiff_high[dofs - block:dofs, dofs + block:] = -next_high
    stiff_low[dofs - block:dofs, dofs + block:] = -next_low

    def early_cols(map_rows, image_rows, cubic_rows):
        map_high, map_low = split(map_rows)
        image_high, image_low = split(image_rows)
        both_high = jnp.concatenate([map_high, image_high], axis=0).astype(F32)
        both_low = jnp.concatenate([map_low, image_low], axis=0).astype(F32)
        rows = jnp.concatenate([both_high, both_high, both_low, pad_rows(cubic_rows, 32)], axis=0)
        cols = jnp.transpose(rows)
        return cols.astype(BF16), cols[:, 96:97]

    def late_cols(second_rows, image_rows):
        second_high, second_low = split(second_rows)
        image_high, image_low = split(image_rows)
        return jnp.transpose(jnp.concatenate([
            second_high, second_high, second_low, image_high, image_high, image_low,
            jnp.zeros((32, second_rows.shape[1]), BF16),
        ], axis=0))

    own_early, own_cubic = early_cols(maps, image_map, cubic)
    own_late = late_cols(second_map, jnp.zeros_like(second_map))
    arrive(point_copies)
    received = collect(in_points)
    flag = received[comps:comps + 1]
    strain = jnp.where(iota((16, columns), 0) < comps, received, 0.0)
    strain_high, strain_low = split(strain)
    hard = own_cubic * flag

    arrive(ghost_copies)
    prev_rows = unpack(base_in[...])
    last_rows = last_in[...]
    last_high, last_low = split(jnp.concatenate([
        last_rows[:, :dofs - LANES],
        last_rows[:, dofs - LANES:] + jnp.concatenate([jnp.zeros_like(own_spring), own_spring], axis=1),
    ], axis=1))
    ghost_early, ghost_cubic = early_cols(
        jnp.concatenate([prev_rows[0:16], next_map], axis=1),
        jnp.concatenate([
            jnp.zeros((16, block), F32), prev_rows[16:32, block:dofs - block], prev_image, next_image,
        ], axis=1),
        jnp.concatenate([prev_rows[32:40], next_in[32:40, :block]], axis=1),
    )
    ghost_hard = ghost_cubic * flag

    arrive(gram_copies)
    gram = gathered(gram_buf)
    form_high, form_low = split(jnp.concatenate(
        [gram[:, 0:16], gram[:, 16:32], gram[:, 32:48], gram[:, 48:64]], axis=0
    ))
    wide = dot(
        jnp.concatenate([form_high, form_low], axis=0), jnp.concatenate([strain_high, strain_low], axis=1)
    )
    forms = wide[:64, :columns] + (wide[:64, columns:] + wide[64:, :columns])
    norm = col_sum(forms[0:16] * strain)
    curve = col_sum(forms[16:32] * strain)
    third = col_sum(forms[32:48] * strain)
    fourth = col_sum(forms[48:64] * strain)

    def second_step(norm, curve, left_norm, left_curve, cross):
        ratio = left_norm / (norm + EPSILON)
        next_curve = left_curve + ratio * (2.0 * cross + ratio * curve)
        next_curve = jnp.maximum(next_curve, 0.09 * left_norm)
        next_len = left_norm / (next_curve + EPSILON)
        return next_len, next_len * ratio

    step_len = norm / (curve + EPSILON)
    left_norm = jnp.maximum(norm - step_len * (2.0 * curve - step_len * third), 0.0)
    left_curve = curve - step_len * (2.0 * third - step_len * fourth)
    cross = curve - step_len * third
    next_len, carried = second_step(norm, curve, left_norm, left_curve, cross)
    along = step_len + carried + next_len
    across = next_len * step_len
    weights = jnp.concatenate([
        jnp.concatenate([along * strain, -across * strain, jnp.zeros_like(strain)], axis=0),
        jnp.concatenate([strain, -along * strain, across * strain], axis=0),
    ], axis=1)
    weight_high, weight_low = split(weights)
    arrive(map_copies)
    ghost_late = late_cols(
        jnp.concatenate([map_in[:, :dofs], head_in[:, :block]], axis=1),
        jnp.concatenate([map_in[:, dofs:dofs + block], jnp.zeros((16, dofs), F32)], axis=1),
    )
    blank = jnp.zeros((32, 2 * columns), BF16)
    both = dot(
        jnp.concatenate([
            jnp.concatenate([own_early, own_late], axis=1), jnp.concatenate([ghost_early, ghost_late], axis=1),
        ], axis=0),
        jnp.concatenate([
            weight_high[:32], weight_low[:32], weight_high[:32], blank,
            weight_high[32:], weight_low[32:], weight_high[32:],
            weight_high[16:32], weight_low[16:32], weight_high[16:32], blank,
        ], axis=0),
    )
    solved = both[:dofs, :columns]
    hard_square = hard * solved * solved
    tangent = 3.0 * hard_square
    residue = both[:dofs, columns:] - hard_square * solved
    ghost_solved = both[dofs:, :columns]
    ghost_square = ghost_hard * ghost_solved * ghost_solved
    ghost = both[dofs:, columns:] - ghost_square * ghost_solved
    own_product = apply_split(
        stiff_high[...], stiff_low[...], jnp.concatenate([residue, ghost[dofs - block:]], axis=0)
    )
    last_product = apply_split(last_high, last_low, ghost[:dofs])
    image = own_product[:dofs] + tangent * residue
    last_residue = ghost[dofs - block:dofs]
    last_image = (
        last_product + 3.0 * ghost_square[dofs - block:dofs] * last_residue - own_product[dofs + 16:]
    )
    image_product = apply_split(
        stiff_high[:dofs + 16, :], stiff_low[:dofs + 16, :],
        jnp.concatenate([image, 2.0 * last_image, jnp.zeros_like(last_image)], axis=0),
    )

    mean_high, mean_low = split(gram[:, 64:112])
    mean_out[...] = (
        dot(mean_high, weight_high[:, :columns])
        + (dot(mean_high, weight_low[:, :columns]) + dot(mean_low, weight_high[:, :columns]))
    )
    mean_copy = hand_over(mean_out, mean_in, part, parts)

    scaled = SCALE * image
    length = jnp.sqrt(col_sum(scaled * scaled))
    inverse = jnp.where(length > 0.0, SCALE / jnp.where(length > 0.0, length, 1.0), 0.0)
    length = length * (1.0 / SCALE)
    unit = inverse * image
    along_unit = col_sum(residue * unit)
    rest = residue - along_unit * unit
    form_unit = inverse * (image_product[:dofs] + tangent * image)
    form_rest = jnp.concatenate([
        image[:block] - apply_split(own_high, own_low, last_residue), image[block:dofs - block],
        image[dofs - block:] + apply_split(next_high, next_low, ghost[dofs:]),
    ], axis=0) - along_unit * form_unit
    sum_out[...] = pad_rows(jnp.concatenate([
        length, along_unit, col_sum(rest * rest),
        col_sum(rest * form_rest), col_sum(rest * form_unit + unit * form_rest), col_sum(unit * form_unit),
        own_product[dofs:dofs + comps], image_product[dofs:dofs + comps],
    ], axis=0), sum_out.shape[0])
    twin_copies = [mean_copy]
    for step in range(parts):
        peer = lax.rem(part + step, parts)
        twin_copies.append(hand_over(sum_out, twin_buf.at[part], peer, step))
    sum_buf[part] = sum_out[:8]
    sum_copies = share(sum_buf, sum_send, sum_recv)
    sends += sum_copies + twin_copies
    def lengths(sums):
        norm = sum(each[2:3] + each[1:2] * each[1:2] for each in sums)
        curve = sum(each[0:1] * each[1:2] for each in sums)
        step_len = norm / (curve + EPSILON)
        left_norm, left_curve, cross = 0.0, 0.0, 0.0
        for each in sums:
            beyond = step_len * each[0:1] - each[1:2]
            left_norm = left_norm + (each[2:3] + beyond * beyond)
            left_curve = left_curve + (each[3:4] - beyond * (each[4:5] - beyond * each[5:6]))
            cross = cross - beyond * each[0:1]
        next_len, carried = second_step(norm, curve, left_norm, left_curve, cross)
        return step_len, next_len, step_len + carried

    arrive(twin_copies)
    sums = [twin_buf[other] for other in range(parts)]
    means = sum(sums[1:], sums[0])[6:]
    step_len, next_len, along = lengths(sums)
    total = (
        mean_in[:comps] + along * means[:comps]
        + next_len * (means[:comps] - step_len * means[comps:2 * comps])
    )

    out_rows[...] = pad_rows(total, 16)
    row_copies = exchange(out_rows, in_rows, twin, row_send, row_recv)
    in_rows[twin] = out_rows[...]
    arrive(sum_copies)
    step_len, next_len, along = lengths([sum_buf[other] for other in range(parts)])
    field_ref[0] = solved + along * residue + next_len * (residue - step_len * image)
    for copy in sends:
        copy.wait_send()
    arrive(row_copies)
    back = collect(in_rows)
    back_high, back_low = split(back)
    back_rest = (back - back_high.astype(F32) - back_low.astype(F32)).astype(BF16)
    picked = dot(jnp.concatenate([back_high, back_low, back_rest], axis=0), select.astype(BF16))
    stress_ref[...] = (picked[:16] + (picked[16:32] + picked[32:]))[:comps]
    for copy in row_copies:
        copy.wait_send()


def place(stress_ref, field_ref, stress_out, field_out, sem):
    first = pltpu.make_async_copy(field_ref, field_out, sem.at[0])
    second = pltpu.make_async_copy(stress_ref, stress_out, sem.at[1])
    first.start()
    second.start()
    first.wait()
    second.wait()


def solution(mesh):
    groups, parts = mesh.shape["macro"], mesh.shape["rve"]

    def shards(deform, plastic, route, stiff, cubic, coupling, conn, iface, load_map, average_map):
        comps, points = deform.shape
        blocks, block = coupling.shape[1], coupling.shape[3]
        dofs = blocks * block
        capacity = 2 * points // groups
        columns = groups * capacity
        sum_rows = -(-(6 + 2 * comps) // 8) * 8
        base_rows = -(-(2 * comps + 1) // 8) * 8
        vmem = pl.BlockSpec(memory_space=pltpu.VMEM)
        hbm = pl.BlockSpec(memory_space=pltpu.HBM)
        dma = pltpu.SemaphoreType.DMA
        stress, field = pl.pallas_call(
            functools.partial(kernel, groups, parts, capacity),
            out_shape=(
                pltpu.VMEM((comps, points), F32),
                pltpu.VMEM((1, dofs, columns), F32),
            ),
            in_specs=[hbm] * 6 + [pl.BlockSpec(memory_space=pltpu.SMEM)] + [hbm] * 3,
            out_specs=(vmem, vmem),
            scratch_shapes=[
                pltpu.VMEM(deform.shape, F32),
                pltpu.VMEM((1, points), jnp.int32),
                pltpu.VMEM((1, points), jnp.int32),
                pltpu.VMEM((1, dofs), F32),
                pltpu.VMEM((1, dofs), F32),
                pltpu.VMEM(coupling.shape, F32),
                pltpu.VMEM(iface.shape, F32),
                pltpu.VMEM((comps, 1, dofs), F32),
                pltpu.VMEM((comps, 1, dofs), F32),
                pltpu.VMEM((dofs, dofs), F32),
                pltpu.VMEM((dofs + 16 + block, dofs + 2 * block), BF16),
                pltpu.VMEM((dofs + 16 + block, dofs + 2 * block), BF16),
                pltpu.VMEM((16, columns), F32),
                pltpu.VMEM((groups, 16, columns), F32),
                pltpu.VMEM((40 + block // 2, LANES), F32),
                pltpu.VMEM((40, LANES), F32),
                pltpu.VMEM((40 + block // 2, LANES), F32),
                pltpu.VMEM((base_rows, dofs), F32),
                pltpu.VMEM((base_rows, dofs), F32),
                pltpu.VMEM((block, dofs), F32),
                pltpu.VMEM((16, dofs + LANES), F32),
                pltpu.VMEM((16, dofs + LANES), F32),
                pltpu.VMEM((16, LANES), F32),
                pltpu.VMEM((16, LANES), F32),
                pltpu.VMEM((parts, 16, LANES), F32),
                pltpu.VMEM((sum_rows, columns), F32),
                pltpu.VMEM((parts, 8, columns), F32),
                pltpu.VMEM((parts, sum_rows, columns), F32),
                pltpu.VMEM((16, columns), F32),
                pltpu.VMEM((16, columns), F32),
                pltpu.VMEM((16, columns), F32),
                pltpu.VMEM((groups, 16, columns), F32),
                dma((9,)),
                dma((groups - 1,)), dma((groups - 1,)),
                dma((2,)), dma((2,)),
                dma((4,)), dma((4,)),
                dma((parts - 1,)), dma((parts - 1,)),
                dma((parts - 1,)), dma((parts - 1,)),
                dma((parts + 1,)), dma((parts + 1,)),
                dma((groups - 1,)), dma((groups - 1,)),
            ],
            compiler_params=pltpu.CompilerParams(
                collective_id=0, has_side_effects=True, vmem_limit_bytes=60 * 1024 * 1024
            ),
        )(
            deform, plastic[None], route[None], stiff, cubic, coupling,
            jnp.transpose(conn, (0, 2, 1)), iface,
            jnp.transpose(load_map, (1, 0, 2)), jnp.transpose(average_map, (1, 0, 2)),
        )
        return pl.pallas_call(
            place,
            out_shape=(
                jax.ShapeDtypeStruct((comps, points), F32),
                jax.ShapeDtypeStruct((1, dofs, columns), F32),
            ),
            in_specs=[vmem, vmem], out_specs=(hbm, hbm),
            scratch_shapes=[dma((2,))],
        )(*(pltpu.with_memory_space_constraint(x, pltpu.VMEM) for x in (stress, field)))

    return jax.shard_map(
        shards,
        mesh=mesh,
        in_specs=(
            P(None, "macro"),
            P("macro"),
            P("macro"),
            P("macro", "rve"),
            P("macro", "rve"),
            P("macro", "rve", None, None, None),
            P("macro", "rve", None),
            P("macro", "rve", None),
            P("macro", None, "rve"),
            P("macro", None, "rve"),
        ),
        out_specs=(P(None, "macro"), P("macro", "rve", None)),
        check_vma=False,
    )
```
